32 devices in a mesh: group: 2 (over y), expert: 4 (over x, core), seq: 4 (over z).
Axes of the slice: x: 2, y: 2, z: 4, core: 2. Of those that a mesh axis runs over, the one named last changes fastest.
Arguments:
- tokens: bfloat16 [4096, 2048], P(('group', 'expert', 'seq')), parts along dimension 0, may hold values from -6 to 6
- grad_out: bfloat16 [4096, 2048], P(('group', 'expert', 'seq')), parts along dimension 0, may hold values from -6 to 6
- probs: bfloat16 [4096, 8], P(('group', 'expert', 'seq')), parts along dimension 0, may hold values from 0.049804688 to 0.5
- routes: int32 [4096, 8], P(('group', 'expert')), parts along dimension 0, may hold values from 0 to 15, all different within a row; in each aligned block of 128 rows (0 to 127, 128 to 255, ...) at most 80 rows name the same one
- w_gate: bfloat16 [16, 2048, 384], P(('expert', 'seq')), may hold values from -0.3125 to 0.3125
- w_up: bfloat16 [16, 2048, 384], P(('expert', 'seq')), may hold values from -0.3125 to 0.3125
- w_down: bfloat16 [16, 384, 2048], P(('expert', 'seq')), may hold values from -0.125 to 0.125
- gate_pre: bfloat16 [32, 1280, 384], P(('group', 'expert', 'seq')), parts along dimension 0, may hold values from -6 to 6
- up_pre: bfloat16 [32, 1280, 384], P(('group', 'expert', 'seq')), parts along dimension 0, may hold values from -0.59765625 to 0.59765625
Outputs:
- grad_tokens: bfloat16 [4096, 2048], P(('group', 'expert', 'seq')), parts along dimension 0
- grad_probs: bfloat16 [4096, 8], P(('group', 'expert', 'seq')), parts along dimension 0
- grad_gate: bfloat16 [32, 2048, 384], P(('group', 'expert', 'seq')), parts along dimension 0
- grad_up: bfloat16 [32, 2048, 384], P(('group', 'expert', 'seq')), parts along dimension 0
- grad_down: bfloat16 [32, 384, 2048], P(('group', 'expert', 'seq')), parts along dimension 0
The draws below stay inside these ranges and needn't reach their ends.
There are 2 independent parts, one for each index of `group`. The reference program is written for one: setup_inputs(seed, part) draws one part's arguments, and reference() takes and returns one part's arrays. A program takes and returns all parts, laid end to end along the dimension named above; an argument that names none is the same for every part. Nothing has to cross between parts.
Inputs may be any that keep to these rules, and one draw needn't show every extreme that they name: `routes`: each row names 8 different experts; within every aligned block of 128 tokens no expert is named by more than 80 tokens, a bound that some block reaches.
All inputs are finite; a program needn't handle non-finite values.
Results may differ from the reference program's by a relative error of at most 0.006.
Values may be sent and summed in bfloat16 or wider, within the bound.
No kernel may reach another device: no remote copies, remote signals or barrier semaphores. Data moves between devices by JAX's collectives and lax.ppermute only.
A program may use at most 128 MiB of HBM per device.

```python
import math
import jax
import jax.numpy as jnp
import numpy as np
from jax import lax

D = 2048
H = 384
TOP = 8
TOK_DEV = 128
EXPERTS = 16
TOKENS = 2048
MOST = 80
SLOTS = 1280


def steps_of(own_key, extent, pieces, least, top_value):
    def one(axis_at, blocks):
        steps = jax.random.uniform(jax.random.fold_in(jax.random.fold_in(own_key, 6), axis_at), (blocks,), jnp.float32, least / len(pieces), top_value / len(pieces))
        return jnp.repeat(jnp.exp(steps), extent[axis_at] // blocks).reshape((-1,) + (1,) * (len(extent) - axis_at - 1))

    factor_of = one(*pieces[0])
    for cut in pieces[1:]:
        factor_of = factor_of * one(*cut)
    return factor_of


def routed_block(stream_key, own, number, rows, count, top, most, skew):
    order = jax.random.permutation(stream_key, count)
    packed, ordinary = shares(count, rows * top, most, skew, True), shares(count, rows * top, most, skew, False)
    places = jnp.arange(count)

    def named(sizes, turn):
        used = int((sizes > 0).sum())
        fixed = max(1, used // 4)
        passed = fixed + (places - fixed + turn * (used - fixed)) % max(1, count - fixed)
        return jnp.zeros((count,), jnp.int32).at[order[jnp.where(places < fixed, places, passed)]].set(jnp.asarray(sizes, jnp.int32))

    sizes = jnp.where(number % 4 == 0, named(packed, number // 4), named(ordinary, number - number // 4 - 1))
    mixed = jax.random.permutation(jax.random.fold_in(own, 3), count)
    donor, receiver = mixed[0:count // 2 * 2:2], mixed[1:count // 2 * 2:2]
    margin = jnp.minimum(sizes[donor] - 1, most - sizes[receiver]) // 2
    margin = jnp.where((donor == order[0]) | (receiver == order[0]) | (sizes[receiver] == 0), 0, jnp.maximum(margin, 0))
    passed = jax.random.randint(jax.random.fold_in(own, 4), (count // 2,), 0, 1 << 20) % (margin + 1)
    sizes = sizes.at[donor].add(-passed).at[receiver].add(passed)
    items = jnp.searchsorted(jnp.cumsum(sizes), jnp.arange(rows * top), side="right").astype(jnp.int32)
    table = items.reshape(top, rows).T
    table = table[jax.random.permutation(jax.random.fold_in(own, 1), rows)]
    turn = jax.random.randint(jax.random.fold_in(own, 2), (rows, 1), 0, top)
    return jnp.take_along_axis(table, (jnp.arange(top)[None, :] + turn) % top, axis=1)


def shares(count, total, limit, skew, full):
    loads = [(1 << 20) // math.isqrt(grade ** skew) + 1 for grade in range(1, count + 1)]
    largest = limit if full else min(limit, max(-(-total // count), total * loads[0] // sum(loads)))
    least = 1 if total - largest >= count - 1 else 0
    counts, spare = [largest] + [least] * (count - 1), total - largest - least * (count - 1)
    while spare > 0:
        free = [i for i in range(1, count) if counts[i] < largest] or [i for i in range(1, count) if counts[i] < limit]
        mass, budget = sum([loads[i] for i in free]), spare
        for i in free:
            extra = min(limit - counts[i], max(1, budget * loads[i] // mass), spare)
            counts[i] = counts[i] + extra
            spare = spare - extra
    return np.array(counts)


def normal_values(rng, shape, scale, most, cuts=(), kind=jnp.bfloat16):
    values = jax.random.normal(rng, shape, jnp.float32) * scale
    if len(cuts) > 0:
        values = steps_of(rng, shape, cuts, -0.22, 0.18) * values
    return jnp.clip(values, min=-most, max=most).astype(kind)


def setup_inputs(seed: int = 0, part: int = 0) -> dict:
    streams_of = jax.random.split(jax.random.key(seed), 10)
    part_splits = jax.random.split(jax.random.fold_in(streams_of[9], part), 10)
    tokens = normal_values(part_splits[0], (TOKENS, D), 1.0, 6.0, ((0, 16),))
    grad_out = normal_values(part_splits[1], (TOKENS, D), 1.0, 6.0, ((0, 16),))
    probs = jnp.clip(jnp.exp(math.log(0.5) - 2.306499 * jax.random.uniform(part_splits[2], (TOKENS, TOP), jnp.float32) ** steps_of(part_splits[2], (TOKENS, TOP), ((0, 16),), -0.2, 0.2)), 0.049804688, 0.5).astype(jnp.bfloat16)
    routes_keys = jax.random.split(jax.random.fold_in(part_splits[3], 1), TOKENS // TOK_DEV)
    routes_turns = jax.random.permutation(jax.random.fold_in(part_splits[3], 3), TOKENS // TOK_DEV)
    routes = jax.vmap(lambda own, number: routed_block(jax.random.fold_in(part_splits[3], 2), own, number, TOK_DEV, EXPERTS, TOP, MOST, 2))(routes_keys, routes_turns).reshape((TOKENS, TOP))
    w_gate = normal_values(streams_of[4], (EXPERTS, D, H), H ** -0.5, 0.3125, ((0, 16),))
    w_up = normal_values(streams_of[5], (EXPERTS, D, H), H ** -0.5, 0.3125, ((0, 16),))
    w_down = normal_values(streams_of[6], (EXPERTS, H, D), D ** -0.5, 0.125, ((0, 16),))
    gate_pre = normal_values(part_splits[7], (EXPERTS, SLOTS, H), 1.0, 6.0, ((0, 16),))
    up_pre = normal_values(part_splits[8], (EXPERTS, SLOTS, H), 0.1, 0.59765625, ((0, 16),))
    return {"tokens": tokens, "grad_out": grad_out, "probs": probs, "routes": routes, "w_gate": w_gate, "w_up": w_up, "w_down": w_down, "gate_pre": gate_pre, "up_pre": up_pre}


def with_zero(values):
    return jnp.concatenate([values, jnp.zeros((1,) + values.shape[1:], values.dtype)], axis=0)


def expert_backward(rows_x, rows_dy, rows_p, gate_w, up_w, down_w, gate_in, up_in):
    gate_f = gate_in.astype(jnp.float32)
    up_f = up_in.astype(jnp.float32)
    logistic = jax.nn.sigmoid(gate_f)
    active = gate_f * logistic
    hidden = active * up_f
    back_rows = jnp.dot(rows_dy, down_w.T, preferred_element_type=jnp.float32)
    slot_dprob = jnp.sum(back_rows * hidden, axis=1).astype(jnp.bfloat16)
    weight = rows_p.astype(jnp.float32)[:, None]
    d_hidden = weight * back_rows
    d_up = (d_hidden * active).astype(jnp.bfloat16)
    d_gate = (d_hidden * up_f * logistic * (1.0 + gate_f * (1.0 - logistic))).astype(jnp.bfloat16)
    scaled = (weight * hidden).astype(jnp.bfloat16)
    slot_dx = (jnp.dot(d_gate, gate_w.T, preferred_element_type=jnp.float32)
               + jnp.dot(d_up, up_w.T, preferred_element_type=jnp.float32)).astype(jnp.bfloat16)
    grad_gate = jnp.dot(rows_x.T, d_gate, preferred_element_type=jnp.float32).astype(jnp.bfloat16)
    grad_up = jnp.dot(rows_x.T, d_up, preferred_element_type=jnp.float32).astype(jnp.bfloat16)
    grad_down = jnp.dot(scaled.T, rows_dy, preferred_element_type=jnp.float32).astype(jnp.bfloat16)
    return slot_dx, slot_dprob, grad_gate, grad_up, grad_down


def reference(tokens, grad_out, probs, routes, w_gate, w_up, w_down, gate_pre, up_pre):
    blocks = routes.reshape(EXPERTS, TOK_DEV, TOP)
    labels = jnp.arange(EXPERTS, dtype=jnp.int32)
    hits = jnp.sum((blocks[..., None] == labels).astype(jnp.int32), axis=2)
    before = jnp.cumsum(hits, axis=1) - hits
    ranked = jnp.take_along_axis(before, blocks, axis=2)
    source = jnp.arange(EXPERTS, dtype=jnp.int32)[:, None, None]
    slot_place = (blocks * SLOTS + source * MOST + ranked).reshape(TOKENS, TOP)
    entries = TOKENS * TOP
    lookup = jnp.full((EXPERTS * SLOTS,), entries, jnp.int32).at[slot_place.reshape(-1)].set(
        jnp.arange(entries, dtype=jnp.int32))
    padded_x = with_zero(tokens)
    padded_dy = with_zero(grad_out)
    padded_p = with_zero(probs.reshape(-1))

    def one_expert(expert):
        picked = lax.dynamic_slice_in_dim(lookup, expert * SLOTS, SLOTS)
        row_index = picked // TOP
        return expert_backward(padded_x[row_index], padded_dy[row_index], padded_p[picked],
                               w_gate[expert], w_up[expert], w_down[expert],
                               gate_pre[expert], up_pre[expert])

    slot_dx, slot_dprob, grad_gate, grad_up, grad_down = lax.map(
        one_expert, jnp.arange(EXPERTS, dtype=jnp.int32))
    flat_dx = slot_dx.reshape(EXPERTS * SLOTS, D)
    summed = jnp.zeros((TOKENS, D), jnp.float32)
    for column in range(TOP):
        summed = summed + flat_dx[slot_place[:, column]].astype(jnp.float32)
    grad_tokens = summed.astype(jnp.bfloat16)
    grad_probs = slot_dprob.reshape(-1)[slot_place]
    return grad_tokens, grad_probs, grad_gate, grad_up, grad_down
```

```python
import functools

import jax
import jax.numpy as jnp
from jax import lax
from jax.experimental import pallas as pl
from jax.experimental.pallas import tpu as pltpu
from jax.sharding import PartitionSpec as P


def with_zero(values):
    return jnp.concatenate([values, jnp.zeros((1,) + values.shape[1:], values.dtype)], axis=0)


def block_positions(blocks, experts, slot_cap):
    labels = jnp.arange(experts, dtype=jnp.int32)
    hits = jnp.sum((blocks[..., None] == labels).astype(jnp.int32), axis=-2)
    before = jnp.cumsum(hits, axis=-2) - hits
    ranked = jnp.take_along_axis(before, blocks, axis=-1)
    return blocks * slot_cap + ranked


def invert(places, length):
    entries = places.shape[0]
    return (
        jnp.full((length,), entries, jnp.int32).at[places].set(jnp.arange(entries, dtype=jnp.int32))
    )


def expert_backward(rows_x, rows_dy, rows_p, gate_w, up_w, down_w, gate_in, up_in):
    gate_f = gate_in.astype(jnp.float32)
    up_f = up_in.astype(jnp.float32)
    logistic = jax.nn.sigmoid(gate_f)
    active = gate_f * logistic
    hidden = active * up_f
    back_rows = jnp.dot(rows_dy, down_w.T, preferred_element_type=jnp.float32)
    slot_dprob = jnp.sum(back_rows * hidden, axis=1).astype(jnp.bfloat16)
    weight = rows_p.astype(jnp.float32)[:, None]
    d_hidden = weight * back_rows
    d_up = (d_hidden * active).astype(jnp.bfloat16)
    d_gate = (d_hidden * up_f * logistic * (1.0 + gate_f * (1.0 - logistic))).astype(jnp.bfloat16)
    scaled = (weight * hidden).astype(jnp.bfloat16)
    slot_dx = (
        jnp.dot(d_gate, gate_w.T, preferred_element_type=jnp.float32)
        + jnp.dot(d_up, up_w.T, preferred_element_type=jnp.float32)
    ).astype(jnp.bfloat16)
    grad_gate = jnp.dot(rows_x.T, d_gate, preferred_element_type=jnp.float32).astype(jnp.bfloat16)
    grad_up = jnp.dot(rows_x.T, d_up, preferred_element_type=jnp.float32).astype(jnp.bfloat16)
    grad_down = jnp.dot(scaled.T, rows_dy, preferred_element_type=jnp.float32).astype(jnp.bfloat16)
    return (slot_dx, slot_dprob, grad_gate, grad_up, grad_down)


def exchange_local(tokens, grad_out, probs, routes, w_gate, w_up, w_down, gate_pre, up_pre):
    seq_count = lax.axis_size("seq")
    expert_count = lax.axis_size("expert")
    experts = seq_count * expert_count
    token_count = tokens.shape[0]
    chosen = probs.shape[1]
    width = tokens.shape[1]
    slot_cap = gate_pre.shape[1] // experts
    seq_place = lax.axis_index("seq")
    places = block_positions(routes.reshape(seq_count, token_count, chosen), experts, slot_cap)
    own_places = lax.dynamic_index_in_dim(places, seq_place, 0, keepdims=False)
    lookup = invert(own_places.reshape(-1), experts * slot_cap)
    row_index = lookup // chosen
    send_x = with_zero(tokens)[row_index].reshape(experts, slot_cap, width)
    send_dy = with_zero(grad_out)[row_index].reshape(experts, slot_cap, width)
    send_p = with_zero(probs.reshape(-1))[lookup].reshape(experts, slot_cap)
    got_x, got_dy, got_p = (
        lax.all_to_all(send_x, ("expert", "seq"), split_axis=0, concat_axis=0, tiled=True),
        lax.all_to_all(send_dy, ("expert", "seq"), split_axis=0, concat_axis=0, tiled=True),
        lax.all_to_all(send_p, ("expert", "seq"), split_axis=0, concat_axis=0, tiled=True),
    )
    slot_dx, slot_dprob, grad_gate, grad_up, grad_down = expert_backward(
        got_x.reshape(-1, width),
        got_dy.reshape(-1, width),
        got_p.reshape(-1),
        w_gate[0],
        w_up[0],
        w_down[0],
        gate_pre[0],
        up_pre[0],
    )
    back_x, back_p = (
        lax.all_to_all(
            slot_dx.reshape(experts, slot_cap, width),
            ("expert", "seq"),
            split_axis=0,
            concat_axis=0,
            tiled=True,
        ),
        lax.all_to_all(
            slot_dprob.reshape(experts, slot_cap),
            ("expert", "seq"),
            split_axis=0,
            concat_axis=0,
            tiled=True,
        ),
    )
    flat_x = back_x.reshape(-1, width)
    summed = jnp.zeros((token_count, width), jnp.float32)
    for column in range(chosen):
        summed = summed + flat_x[own_places[:, column]].astype(jnp.float32)
    grad_tokens = summed.astype(jnp.bfloat16)
    grad_probs = back_p.reshape(-1)[own_places]
    return (grad_tokens, grad_probs, grad_gate[None], grad_up[None], grad_down[None])


TILE = 512


def dot_nt(a, b):
    return lax.dot_general(a, b, (((1,), (1,)), ((), ())), preferred_element_type=jnp.float32)


def dot_tn(a, b):
    return lax.dot_general(a, b, (((0,), (0,)), ((), ())), preferred_element_type=jnp.float32)


def slot_hits(slot_ref, block, slot_cap):
    slots = slot_ref[block]
    shape = (slot_cap, slots.shape[1])
    return lax.broadcasted_iota(jnp.int32, shape, 0) == jnp.broadcast_to(slots, shape)


def as_bf16(hits):
    return jnp.where(hits, 1.0, 0.0).astype(jnp.bfloat16)


def round_kernel(
    ids_ref, slot_ref, prob_ref, dy0, dy1, dy2, dy3, down_ref, gate_w_ref, up_w_ref, gate_ref, up_ref,
    dx0, dx1, dx2, dx3, rows_ref, dgu_ref, scaled_ref, dprob_ref,
    back_ref,
):
    pieces, results = (dy0, dy1, dy2, dy3), (dx0, dx1, dx2, dx3)
    slot_cap, hid = gate_ref.shape[1:]
    width = dy0.shape[1]
    blocks = [ids_ref[i] for i in range(4)]
    hits = [slot_hits(slot_ref, block, slot_cap) for block in blocks]
    select = [as_bf16(h) for h in hits]
    back_ref[...] = jnp.zeros_like(back_ref)

    def project(step, carry):
        cols = pl.ds(pl.multiple_of(step * TILE, TILE), TILE)
        for i in range(4):
            rows = jnp.dot(select[i], pieces[i][:, cols], preferred_element_type=jnp.float32)
            rows_ref[i * slot_cap:(i + 1) * slot_cap, cols] = rows.astype(jnp.bfloat16)
        back_ref[...] += dot_nt(rows_ref[:, cols], down_ref[:, cols])
        return carry

    lax.fori_loop(0, width // TILE, project, 0)
    for i in range(4):
        span = slice(i * slot_cap, (i + 1) * slot_cap)
        gate_f = gate_ref[blocks[i]].astype(jnp.float32)
        up_f = up_ref[blocks[i]].astype(jnp.float32)
        back_rows = back_ref[span, :]
        probs = jnp.broadcast_to(prob_ref[blocks[i]], hits[i].shape)
        weight = jnp.sum(jnp.where(hits[i], probs, 0.0), axis=1, keepdims=True)
        logistic = jax.nn.sigmoid(gate_f)
        active = gate_f * logistic
        hidden = active * up_f
        dprob = jnp.sum(back_rows * hidden, axis=1, keepdims=True)
        dprob = jnp.broadcast_to(dprob, hits[i].shape)
        dprob_ref[i] = jnp.sum(jnp.where(hits[i], dprob, 0.0), axis=0, keepdims=True)
        d_hidden = weight * back_rows
        slope = logistic * (1.0 + gate_f * (1.0 - logistic))
        dgu_ref[span, :hid] = (d_hidden * up_f * slope).astype(jnp.bfloat16)
        dgu_ref[span, hid:] = (d_hidden * active).astype(jnp.bfloat16)
        scaled_ref[span, :] = (weight * hidden).astype(jnp.bfloat16)

    def unproject(step, carry):
        cols = pl.ds(pl.multiple_of(step * TILE, TILE), TILE)
        slot_dx = dot_nt(dgu_ref[:, :hid], gate_w_ref[cols, :])
        slot_dx = (slot_dx + dot_nt(dgu_ref[:, hid:], up_w_ref[cols, :])).astype(jnp.bfloat16)
        for i in range(4):
            span = slice(i * slot_cap, (i + 1) * slot_cap)
            results[i][:, cols] = dot_tn(select[i], slot_dx[span, :]).astype(jnp.bfloat16)
        return carry

    lax.fori_loop(0, width // TILE, unproject, 0)


def round_backward(ids, slots, probs, pieces, down_w, gate_w, up_w, gate_in, up_in):
    rows, width = pieces[0].shape
    slot_cap, hid = gate_in.shape[1:]
    taken = 4 * slot_cap
    half = jnp.bfloat16
    vmem = pl.BlockSpec(memory_space=pltpu.VMEM)
    flops = 2 * taken * width * (3 * hid + 2 * rows)
    moved = 2 * (3 * width * hid + 8 * rows * width + taken * (width + 5 * hid))
    out = pl.pallas_call(
        round_kernel,
        out_shape=[jax.ShapeDtypeStruct((rows, width), half)] * 4
        + [
            jax.ShapeDtypeStruct((taken, width), half),
            jax.ShapeDtypeStruct((taken, 2 * hid), half),
            jax.ShapeDtypeStruct((taken, hid), half),
            jax.ShapeDtypeStruct((4, 1, rows), jnp.float32),
        ],
        in_specs=[pl.BlockSpec(memory_space=pltpu.SMEM)] + [vmem] * 11,
        out_specs=[vmem] * 8,
        scratch_shapes=[pltpu.VMEM((taken, hid), jnp.float32)],
        compiler_params=pltpu.CompilerParams(vmem_limit_bytes=48 << 20),
        cost_estimate=pl.CostEstimate(flops=flops, bytes_accessed=moved, transcendentals=taken * hid),
    )(ids, slots, probs, *pieces, down_w, gate_w, up_w, gate_in, up_in)
    return out[:4], out[4], out[5], out[6], out[7]


def weight_kernel(rounds, slot_cap, ids_ref, slot_ref, *refs):
    count = 4 * rounds
    pieces, rows = refs[:count], refs[count:count + rounds]
    dgu, scaled = refs[count + rounds:count + 2 * rounds], refs[count + 2 * rounds:count + 3 * rounds]
    gate_out, up_out, down_out, all_x, all_dy, all_dgu, all_scaled = refs[count + 3 * rounds:]
    taken = 4 * slot_cap
    hid = gate_out.shape[1]

    @pl.when(pl.program_id(0) == 0)
    def _():
        for r in range(rounds):
            all_dgu[r * taken:(r + 1) * taken, :] = dgu[r][...]
            all_scaled[r * taken:(r + 1) * taken, :] = scaled[r][...]

    for i in range(count):
        select = as_bf16(slot_hits(slot_ref, ids_ref[i], slot_cap))
        picked = jnp.dot(select, pieces[i][...], preferred_element_type=jnp.float32)
        all_x[i * slot_cap:(i + 1) * slot_cap, :] = picked.astype(jnp.bfloat16)
    for r in range(rounds):
        all_dy[r * taken:(r + 1) * taken, :] = rows[r][...]
    grads = dot_tn(all_x[...], all_dgu[...])
    gate_out[...] = grads[:, :hid].astype(jnp.bfloat16)
    up_out[...] = grads[:, hid:].astype(jnp.bfloat16)
    down_out[...] = dot_tn(all_scaled[...], all_dy[...]).astype(jnp.bfloat16)


def weight_grads(ids, slots, pieces, rows, dgu, scaled, slot_cap):
    rounds, count = len(rows), len(pieces)
    size, width = pieces[0].shape
    taken, hid = scaled[0].shape
    half = jnp.bfloat16

    def columns(height):
        return pl.BlockSpec((height, TILE), lambda i: (0, i))

    def whole(shape):
        return pl.BlockSpec(shape, lambda i: (0,) * len(shape))

    total = rounds * taken
    flops = 2 * total * width * (3 * hid + size)
    moved = 2 * (count * size * width + total * (width + 3 * hid) + 3 * width * hid)
    return pl.pallas_call(
        functools.partial(weight_kernel, rounds, slot_cap),
        grid=(width // TILE,),
        out_shape=[
            jax.ShapeDtypeStruct((width, hid), half),
            jax.ShapeDtypeStruct((width, hid), half),
            jax.ShapeDtypeStruct((hid, width), half),
        ],
        in_specs=[pl.BlockSpec(memory_space=pltpu.SMEM), whole(slots.shape)]
        + [columns(size)] * count
        + [columns(taken)] * rounds
        + [whole((taken, 2 * hid))] * rounds
        + [whole((taken, hid))] * rounds,
        out_specs=[
            pl.BlockSpec((TILE, hid), lambda i: (i, 0)),
            pl.BlockSpec((TILE, hid), lambda i: (i, 0)),
            columns(hid),
        ],
        scratch_shapes=[
            pltpu.VMEM((total, TILE), half),
            pltpu.VMEM((total, TILE), half),
            pltpu.VMEM((total, 2 * hid), half),
            pltpu.VMEM((total, hid), half),
        ],
        compiler_params=pltpu.CompilerParams(vmem_limit_bytes=56 << 20),
        cost_estimate=pl.CostEstimate(flops=flops, bytes_accessed=moved, transcendentals=0),
    )(ids, slots, *pieces, *rows, *dgu, *scaled)


class Links:
    def __init__(self, depth):
        self.depth, self.arrived = depth, []

    def send(self, value, axis, pairs):
        if len(self.arrived) >= self.depth:
            value = lax.optimization_barrier((value, self.arrived[-self.depth]))[0]
        got = lax.ppermute(value, axis, pairs)
        self.arrived.append(got)
        return got


def gather_local(tokens, grad_out, probs, routes, w_gate, w_up, w_down, gate_pre, up_pre):
    seq_count = lax.axis_size("seq")
    experts = seq_count * lax.axis_size("expert")
    token_count, width = tokens.shape
    chosen = probs.shape[1]
    slot_cap = gate_pre.shape[1] // experts
    seq_place, expert_place = lax.axis_index("seq"), lax.axis_index("expert")
    core_pairs = [(i, i ^ 1) for i in range(4)]
    side_pairs = [(i, i ^ 2) for i in range(4)]
    shifts = sorted(range(seq_count), key=lambda s: (min(s, seq_count - s), s))
    side, line = Links(2), Links(2)

    def shift(value, by):
        return line.send(value, "seq", [(i, (i + by) % seq_count) for i in range(seq_count)])

    def across(value):
        return side.send(value, "expert", side_pairs)

    def other_core(value):
        return lax.ppermute(value, "expert", core_pairs)

    def block_of(s):
        place = (seq_place - s) % seq_count
        return [(expert_place ^ flip) * seq_count + place for flip in (0, 2, 1, 3)]

    ids = {s: jnp.stack(block_of(s)).astype(jnp.int32) for s in shifts}

    dy, x = {0: grad_out}, {0: tokens}
    dy_side, x_side = {}, {}
    for s in shifts[1:3]:
        dy[s] = shift(grad_out, s)
    dy_side[0] = across(grad_out)
    x_side[0] = across(tokens)

    own_routes = lax.dynamic_slice_in_dim(routes, seq_place * token_count, token_count, 0)
    labels = jnp.arange(experts, dtype=jnp.int32)
    match = own_routes[:, :, None] == labels
    hits = jnp.sum(match.astype(jnp.int32), axis=1)
    before = jnp.cumsum(hits, axis=0) - hits
    slot_of = jnp.where(hits > 0, before, -1).astype(jnp.bfloat16)
    prob_of = jnp.sum(jnp.where(match, probs[:, :, None], 0), axis=1).astype(jnp.bfloat16)
    info = jnp.stack([slot_of.T, prob_of.T], axis=1)
    info = lax.all_to_all(info, ("expert", "seq"), split_axis=0, concat_axis=0, tiled=True)
    slots = info[:, :1, :].astype(jnp.int32)
    probs_in = info[:, 1:, :].astype(jnp.float32)

    gate_in = gate_pre.reshape(experts, slot_cap, -1)
    up_in = up_pre.reshape(experts, slot_cap, -1)
    for s in shifts[3:]:
        dy[s] = shift(grad_out, s)
    rows, dgu, scaled, dprob, own, away, sums = {}, {}, {}, {}, {}, {}, {}

    def start_return(s):
        pieces = (dy[s], dy_side[s], other_core(dy[s]), other_core(dy_side[s]))
        dx, rows[s], dgu[s], scaled[s], dprob[s] = round_backward(
            ids[s], slots, probs_in, pieces, w_down[0], w_gate[0], w_up[0], gate_in, up_in
        )
        own[s] = (dx[0], other_core(dx[2]))
        away[s] = add(dx[1], other_core(dx[3]))

    def add(*terms):
        total = terms[0].astype(jnp.float32)
        for term in terms[1:]:
            total = total + term.astype(jnp.float32)
        return total.astype(jnp.bfloat16)

    for s in shifts[1:]:
        dy_side[s] = across(dy[s])
    for s in shifts[1:]:
        x[s] = shift(tokens, s)
    for s in shifts:
        start_return(s)
        arrived = across(away[s])
        sums[s] = (*own[s], arrived)
        if s:
            sums[s] = (shift(add(*sums[s]), -s),)
    for s in shifts[1:]:
        x_side[s] = across(x[s])
    grad_tokens = add(*[term for s in shifts for term in sums[s]])

    pieces = []
    for s in shifts:
        pieces += [x[s], x_side[s], other_core(x[s]), other_core(x_side[s])]
    grad_gate, grad_up, grad_down = weight_grads(
        jnp.concatenate([ids[s] for s in shifts]),
        slots,
        pieces,
        [rows[s] for s in shifts],
        [dgu[s] for s in shifts],
        [scaled[s] for s in shifts],
        slot_cap,
    )
    order = jnp.concatenate([ids[s] for s in shifts])
    dense = jnp.concatenate([dprob[s] for s in shifts], axis=0)[:, 0, :]
    placed = jnp.sum(jnp.where((labels[:, None] == order)[:, :, None], dense, 0.0), axis=1)
    back = lax.all_to_all(
        placed.astype(jnp.bfloat16)[:, None, :], ("expert", "seq"), split_axis=0, concat_axis=0, tiled=True
    )
    grad_probs = jnp.sum(jnp.where(match, back[:, 0, :].T[:, None, :], 0), axis=2).astype(jnp.bfloat16)
    return (grad_tokens, grad_probs, grad_gate[None], grad_up[None], grad_down[None])


def local(tokens, grad_out, probs, routes, w_gate, w_up, w_down, gate_pre, up_pre):
    experts = lax.axis_size("seq") * lax.axis_size("expert")
    gathers = experts * tokens.shape[0] <= 2 * gate_pre.shape[1]
    plan = gather_local if gathers and lax.axis_size("expert") == 4 else exchange_local
    return plan(tokens, grad_out, probs, routes, w_gate, w_up, w_down, gate_pre, up_pre)


def solution(mesh):
    return jax.shard_map(
        local,
        mesh=mesh,
        in_specs=(
            P(("group", "expert", "seq"), None),
            P(("group", "expert", "seq"), None),
            P(("group", "expert", "seq"), None),
            P(("group", "expert"), None),
            P(("expert", "seq"), None, None),
            P(("expert", "seq"), None, None),
            P(("expert", "seq"), None, None),
            P(("group", "expert", "seq"), None, None),
            P(("group", "expert", "seq"), None, None),
        ),
        out_specs=(
            P(("group", "expert", "seq"), None),
            P(("group", "expert", "seq"), None),
            P(("group", "expert", "seq"), None, None),
            P(("group", "expert", "seq"), None, None),
            P(("group", "expert", "seq"), None, None),
        ),
        check_vma=False,
    )
```

```python
import functools

import jax
import jax.numpy as jnp
from jax import lax
from jax.experimental import pallas as pl
from jax.experimental.pallas import tpu as pltpu
from jax.sharding import PartitionSpec as P


def with_zero(values):
    return jnp.concatenate([values, jnp.zeros((1,) + values.shape[1:], values.dtype)], axis=0)


def block_positions(blocks, experts, slot_cap):
    labels = jnp.arange(experts, dtype=jnp.int32)
    hits = jnp.sum((blocks[..., None] == labels).astype(jnp.int32), axis=-2)
    before = jnp.cumsum(hits, axis=-2) - hits
    ranked = jnp.take_along_axis(before, blocks, axis=-1)
    return blocks * slot_cap + ranked


def invert(places, length):
    entries = places.shape[0]
    return (
        jnp.full((length,), entries, jnp.int32).at[places].set(jnp.arange(entries, dtype=jnp.int32))
    )


def expert_backward(rows_x, rows_dy, rows_p, gate_w, up_w, down_w, gate_in, up_in):
    gate_f = gate_in.astype(jnp.float32)
    up_f = up_in.astype(jnp.float32)
    logistic = jax.nn.sigmoid(gate_f)
    active = gate_f * logistic
    hidden = active * up_f
    back_rows = jnp.dot(rows_dy, down_w.T, preferred_element_type=jnp.float32)
    slot_dprob = jnp.sum(back_rows * hidden, axis=1).astype(jnp.bfloat16)
    weight = rows_p.astype(jnp.float32)[:, None]
    d_hidden = weight * back_rows
    d_up = (d_hidden * active).astype(jnp.bfloat16)
    d_gate = (d_hidden * up_f * logistic * (1.0 + gate_f * (1.0 - logistic))).astype(jnp.bfloat16)
    scaled = (weight * hidden).astype(jnp.bfloat16)
    slot_dx = (
        jnp.dot(d_gate, gate_w.T, preferred_element_type=jnp.float32)
        + jnp.dot(d_up, up_w.T, preferred_element_type=jnp.float32)
    ).astype(jnp.bfloat16)
    grad_gate = jnp.dot(rows_x.T, d_gate, preferred_element_type=jnp.float32).astype(jnp.bfloat16)
    grad_up = jnp.dot(rows_x.T, d_up, preferred_element_type=jnp.float32).astype(jnp.bfloat16)
    grad_down = jnp.dot(scaled.T, rows_dy, preferred_element_type=jnp.float32).astype(jnp.bfloat16)
    return (slot_dx, slot_dprob, grad_gate, grad_up, grad_down)


def exchange_local(tokens, grad_out, probs, routes, w_gate, w_up, w_down, gate_pre, up_pre):
    seq_count = lax.axis_size("seq")
    expert_count = lax.axis_size("expert")
    experts = seq_count * expert_count
    token_count = tokens.shape[0]
    chosen = probs.shape[1]
    width = tokens.shape[1]
    slot_cap = gate_pre.shape[1] // experts
    seq_place = lax.axis_index("seq")
    places = block_positions(routes.reshape(seq_count, token_count, chosen), experts, slot_cap)
    own_places = lax.dynamic_index_in_dim(places, seq_place, 0, keepdims=False)
    lookup = invert(own_places.reshape(-1), experts * slot_cap)
    row_index = lookup // chosen
    send_x = with_zero(tokens)[row_index].reshape(experts, slot_cap, width)
    send_dy = with_zero(grad_out)[row_index].reshape(experts, slot_cap, width)
    send_p = with_zero(probs.reshape(-1))[lookup].reshape(experts, slot_cap)
    got_x, got_dy, got_p = (
        lax.all_to_all(send_x, ("expert", "seq"), split_axis=0, concat_axis=0, tiled=True),
        lax.all_to_all(send_dy, ("expert", "seq"), split_axis=0, concat_axis=0, tiled=True),
        lax.all_to_all(send_p, ("expert", "seq"), split_axis=0, concat_axis=0, tiled=True),
    )
    slot_dx, slot_dprob, grad_gate, grad_up, grad_down = expert_backward(
        got_x.reshape(-1, width),
        got_dy.reshape(-1, width),
        got_p.reshape(-1),
        w_gate[0],
        w_up[0],
        w_down[0],
        gate_pre[0],
        up_pre[0],
    )
    back_x, back_p = (
        lax.all_to_all(
            slot_dx.reshape(experts, slot_cap, width),
            ("expert", "seq"),
            split_axis=0,
            concat_axis=0,
            tiled=True,
        ),
        lax.all_to_all(
            slot_dprob.reshape(experts, slot_cap),
            ("expert", "seq"),
            split_axis=0,
            concat_axis=0,
            tiled=True,
        ),
    )
    flat_x = back_x.reshape(-1, width)
    summed = jnp.zeros((token_count, width), jnp.float32)
    for column in range(chosen):
        summed = summed + flat_x[own_places[:, column]].astype(jnp.float32)
    grad_tokens = summed.astype(jnp.bfloat16)
    grad_probs = back_p.reshape(-1)[own_places]
    return (grad_tokens, grad_probs, grad_gate[None], grad_up[None], grad_down[None])


TILE = 512
STEP = 1024
VMEM = 60 << 20


def dot_nt(a, b):
    return lax.dot_general(a, b, (((1,), (1,)), ((), ())), preferred_element_type=jnp.float32)


def dot_tn(a, b):
    return lax.dot_general(a, b, (((0,), (0,)), ((), ())), preferred_element_type=jnp.float32)


def slot_hits(slots, slot_cap):
    shape = (slot_cap, slots.shape[1])
    return lax.broadcasted_iota(jnp.int32, shape, 0) == jnp.broadcast_to(slots, shape)


def slots_of(named, before):
    taken = jnp.max(jnp.where(named, 1.0, 0.0), axis=0, keepdims=True)
    ranked = jnp.dot(
        jnp.broadcast_to(taken, named.shape).astype(jnp.bfloat16), before, preferred_element_type=jnp.float32
    )
    return jnp.where(taken > 0.0, ranked[:1], -1.0).astype(jnp.int32)


def as_bf16(hits):
    return jnp.where(hits, 1.0, 0.0).astype(jnp.bfloat16)


def slope_kernel(gate_ref, up_ref, out_ref):
    hid = gate_ref.shape[2]
    gate_f = gate_ref[...].astype(jnp.float32)
    up_f = up_ref[...].astype(jnp.float32)
    logistic = jax.nn.sigmoid(gate_f)
    active = gate_f * logistic
    out_ref[:, :, :hid] = up_f * logistic * (1.0 + gate_f * (1.0 - logistic))
    out_ref[:, :, hid:2 * hid] = active
    out_ref[:, :, 2 * hid:] = active * up_f


def slopes(gate_in, up_in):
    blocks, slot_cap, hid = gate_in.shape
    spec = pl.BlockSpec((2, slot_cap, hid), lambda i: (i, 0, 0))
    return pl.pallas_call(
        slope_kernel,
        grid=(blocks // 2,),
        out_shape=jax.ShapeDtypeStruct((blocks, slot_cap, 3 * hid), jnp.float32),
        in_specs=[spec] * 2,
        out_specs=pl.BlockSpec((2, slot_cap, 3 * hid), lambda i: (i, 0, 0)),
        cost_estimate=pl.CostEstimate(
            flops=10 * gate_in.size, bytes_accessed=16 * gate_in.size, transcendentals=gate_in.size
        ),
    )(gate_in, up_in)


def round_kernel(
    ids_ref, dy0, dy1, dy2, dy3, down_hbm, gate_w_hbm, up_w_hbm, slope_hbm,
    dx0, dx1, dx2, dx3, rows_hbm, dgu_hbm, scaled_hbm, slot_ref,
    dy_ref, info_ref, down_ref, both_w_ref, slope_ref,
    dx_ref, extra_ref, rows_ref, dgu_ref, scaled_ref, in_sems, out_sems,
):
    pieces, results = (dy0, dy1, dy2, dy3), (dx0, dx1, dx2, dx3)
    slot_cap, hid = slope_ref.shape[1], scaled_ref.shape[1]
    height, width = dy0.shape
    count = slot_ref.shape[2]
    taken = 4 * slot_cap
    half = width // 2

    started = []

    def fetch(source, target):
        copy = pltpu.make_async_copy(source, target, in_sems.at[len(started)])
        copy.start()
        started.append(copy)
        return copy

    sent = []

    def send(source, target):
        copy = pltpu.make_async_copy(source, target, out_sems.at[len(sent)])
        copy.start()
        sent.append(copy)

    infos = [fetch(pieces[i].at[count:height, :2 * count], info_ref.at[i]) for i in range(4)]
    tiles = []
    for part in range(2):
        cols = slice(part * half, (part + 1) * half)
        tiles.append(
            [fetch(pieces[i].at[:count, cols], dy_ref.at[i * count:(i + 1) * count, cols]) for i in range(4)]
            + [fetch(down_hbm.at[:, cols], down_ref.at[:, cols])]
        )
    ready = [fetch(slope_hbm.at[ids_ref[i]], slope_ref.at[i]) for i in range(4)]
    weights = []
    for part in range(2):
        span = slice(part * half, (part + 1) * half)
        weights.append(
            [fetch(gate_w_hbm.at[span, :], both_w_ref.at[span, :hid]), fetch(up_w_hbm.at[span, :], both_w_ref.at[span, hid:])]
        )

    expert = ids_ref[4].astype(jnp.float32)
    order = [lax.broadcasted_iota(jnp.int32, (count, count), axis) for axis in (0, 1)]
    before = as_bf16(order[0] < order[1])
    hits, named, probs = [], [], []
    for i in range(4):
        infos[i].wait()
        routes = info_ref[i, :, :count].astype(jnp.float32)
        given = info_ref[i, :, count:].astype(jnp.float32)
        named.append(routes == expert)
        probs.append(jnp.sum(jnp.where(named[i], given, 0.0), axis=0, keepdims=True))
        slot = slots_of(named[i], before)
        slot_ref[i] = slot
        hits.append(slot_hits(slot, slot_cap))
    pairs = []
    for i in (0, 2):
        none = jnp.zeros((slot_cap, count), jnp.bfloat16)
        upper = jnp.concatenate([as_bf16(hits[i]), none], axis=1)
        lower = jnp.concatenate([none, as_bf16(hits[i + 1])], axis=1)
        pairs.append(jnp.concatenate([upper, lower], axis=0))

    back = None
    for part in range(2):
        for copy in tiles[part]:
            copy.wait()
        for start in range(part * half, (part + 1) * half, STEP):
            cols = slice(start, start + STEP)
            for i in range(2):
                span = slice(2 * i * slot_cap, (2 * i + 2) * slot_cap)
                rows = jnp.dot(
                    pairs[i], dy_ref[2 * i * count:(2 * i + 2) * count, cols], preferred_element_type=jnp.float32
                )
                rows_ref[span, cols] = rows.astype(jnp.bfloat16)
            part_back = dot_nt(rows_ref[:, cols], down_ref[:, cols])
            back = part_back if back is None else back + part_back
        cols = slice(part * half, (part + 1) * half)
        send(rows_ref.at[:, cols], rows_hbm.at[:, cols])

    for i in range(4):
        ready[i].wait()
        span = slice(i * slot_cap, (i + 1) * slot_cap)
        back_rows = back[span, :]
        hidden = slope_ref[i, :, 2 * hid:]
        weight = jnp.broadcast_to(probs[i], hits[i].shape)
        weight = jnp.sum(jnp.where(hits[i], weight, 0.0), axis=1, keepdims=True)
        dprob = jnp.sum(back_rows * hidden, axis=1, keepdims=True)
        dprob = jnp.broadcast_to(dprob, hits[i].shape)
        dprob = jnp.sum(jnp.where(hits[i], dprob, 0.0), axis=0, keepdims=True)
        dprob = jnp.where(named[i], jnp.broadcast_to(dprob, named[i].shape), 0.0)
        extra_ref[i, :, :count] = dprob.astype(jnp.bfloat16)
        extra_ref[i, :, count:] = jnp.zeros((height - count, width - count), jnp.bfloat16)
        send(extra_ref.at[i], results[i].at[count:height, :])
        d_hidden = weight * back_rows
        dgu_ref[span, :hid] = (d_hidden * slope_ref[i, :, :hid]).astype(jnp.bfloat16)
        dgu_ref[span, hid:] = (d_hidden * slope_ref[i, :, hid:2 * hid]).astype(jnp.bfloat16)
        scaled_ref[span, :] = (weight * hidden).astype(jnp.bfloat16)
    send(dgu_ref, dgu_hbm)
    send(scaled_ref, scaled_hbm)

    for part in range(2):
        for copy in weights[part]:
            copy.wait()
        for start in range(part * half, (part + 1) * half, STEP):
            cols = slice(start, start + STEP)
            slot_dx = dot_nt(dgu_ref[...], both_w_ref[cols, :]).astype(jnp.bfloat16)
            for i in range(2):
                span = slice(2 * i * slot_cap, (2 * i + 2) * slot_cap)
                both = dot_tn(pairs[i], slot_dx[span, :]).astype(jnp.bfloat16)
                dx_ref[2 * i * count:(2 * i + 2) * count, cols] = both
        cols = slice(part * half, (part + 1) * half)
        for i in (2, 3, 1, 0):
            send(dx_ref.at[i * count:(i + 1) * count, cols], results[i].at[:count, cols])
    for copy in sent:
        copy.wait()


def round_backward(ids, count, pieces, down_w, gate_w, up_w, parts):
    height, width = pieces[0].shape
    slot_cap, hid = parts.shape[1], parts.shape[2] // 3
    taken = 4 * slot_cap
    half = jnp.bfloat16
    anywhere = pl.BlockSpec(memory_space=pl.ANY)
    flops = 2 * taken * width * (3 * hid + 2 * count)
    moved = 2 * (3 * width * hid + 8 * height * width + taken * (width + 5 * hid))
    out = pl.pallas_call(
        round_kernel,
        out_shape=[jax.ShapeDtypeStruct((height, width), half)] * 4
        + [
            jax.ShapeDtypeStruct((taken, width), half),
            jax.ShapeDtypeStruct((taken, 2 * hid), half),
            jax.ShapeDtypeStruct((taken, hid), half),
            jax.ShapeDtypeStruct((4, 1, count), jnp.int32),
        ],
        in_specs=[pl.BlockSpec(memory_space=pltpu.SMEM)] + [anywhere] * 8,
        out_specs=[anywhere] * 7 + [pl.BlockSpec(memory_space=pltpu.VMEM)],
        scratch_shapes=[
            pltpu.VMEM((4 * count, width), half),
            pltpu.VMEM((4, height - count, 2 * count), half),
            pltpu.VMEM(down_w.shape, half),
            pltpu.VMEM((width, 2 * hid), half),
            pltpu.VMEM((4, slot_cap, 3 * hid), jnp.float32),
            pltpu.VMEM((4 * count, width), half),
            pltpu.VMEM((4, height - count, width), half),
            pltpu.VMEM((taken, width), half),
            pltpu.VMEM((taken, 2 * hid), half),
            pltpu.VMEM((taken, hid), half),
            pltpu.SemaphoreType.DMA((22,)),
            pltpu.SemaphoreType.DMA((16,)),
        ],
        compiler_params=pltpu.CompilerParams(vmem_limit_bytes=VMEM),
        cost_estimate=pl.CostEstimate(flops=flops, bytes_accessed=moved, transcendentals=0),
    )(ids, *pieces, down_w, gate_w, up_w, parts)
    return out[:4], out[4], out[5], out[6], out[7]


def weight_kernel(rounds, slot_cap, *refs):
    count = 4 * rounds
    pieces, rows = refs[:count], refs[count:count + rounds]
    dgu, scaled = refs[count + rounds:count + 2 * rounds], refs[count + 2 * rounds:count + 3 * rounds]
    slots = refs[count + 3 * rounds:count + 4 * rounds]
    gate_out, up_out, down_out, all_x, all_dy, all_dgu, all_scaled = refs[count + 4 * rounds:]
    taken = 4 * slot_cap
    hid = gate_out.shape[1]

    @pl.when(pl.program_id(0) == 0)
    def _():
        for r in range(rounds):
            all_dgu[r * taken:(r + 1) * taken, :] = dgu[r][...]
            all_scaled[r * taken:(r + 1) * taken, :] = scaled[r][...]

    for i in range(count):
        select = as_bf16(slot_hits(slots[i // 4][i % 4], slot_cap))
        picked = jnp.dot(select, pieces[i][...], preferred_element_type=jnp.float32)
        all_x[i * slot_cap:(i + 1) * slot_cap, :] = picked.astype(jnp.bfloat16)
    for r in range(rounds):
        all_dy[r * taken:(r + 1) * taken, :] = rows[r][...]
    grads = dot_tn(all_x[...], all_dgu[...])
    gate_out[...] = grads[:, :hid].astype(jnp.bfloat16)
    up_out[...] = grads[:, hid:].astype(jnp.bfloat16)
    down_out[...] = dot_tn(all_scaled[...], all_dy[...]).astype(jnp.bfloat16)


def weight_grads(pieces, rows, dgu, scaled, slots):
    rounds, count = len(rows), len(pieces)
    size, width = pieces[0].shape
    taken, hid = scaled[0].shape
    half = jnp.bfloat16

    def columns(height):
        return pl.BlockSpec((height, TILE), lambda i: (0, i))

    def whole(shape):
        return pl.BlockSpec(shape, lambda i: (0,) * len(shape))

    slot_cap, total = taken // 4, rounds * taken
    flops = 2 * total * width * (3 * hid + size)
    moved = 2 * (count * size * width + total * (width + 3 * hid) + 3 * width * hid)
    return pl.pallas_call(
        functools.partial(weight_kernel, rounds, slot_cap),
        grid=(width // TILE,),
        out_shape=[
            jax.ShapeDtypeStruct((width, hid), half),
            jax.ShapeDtypeStruct((width, hid), half),
            jax.ShapeDtypeStruct((hid, width), half),
        ],
        in_specs=[columns(size)] * count
        + [columns(taken)] * rounds
        + [whole((taken, 2 * hid))] * rounds
        + [whole((taken, hid))] * rounds
        + [whole(slots[0].shape)] * rounds,
        out_specs=[
            pl.BlockSpec((TILE, hid), lambda i: (i, 0)),
            pl.BlockSpec((TILE, hid), lambda i: (i, 0)),
            columns(hid),
        ],
        scratch_shapes=[
            pltpu.VMEM((total, TILE), half),
            pltpu.VMEM((total, TILE), half),
            pltpu.VMEM((total, 2 * hid), half),
            pltpu.VMEM((total, hid), half),
        ],
        compiler_params=pltpu.CompilerParams(vmem_limit_bytes=56 << 20),
        cost_estimate=pl.CostEstimate(flops=flops, bytes_accessed=moved, transcendentals=0),
    )(*pieces, *rows, *dgu, *scaled, *slots)


def after(value, *others):
    return value if not others else lax.optimization_barrier((value, *others))[0]


class Links:
    def __init__(self, depth):
        self.depth, self.arrived = depth, []

    def send(self, value, axis, pairs):
        if len(self.arrived) >= self.depth:
            value = after(value, self.arrived[-self.depth])
        got = lax.ppermute(value, axis, pairs)
        self.arrived.append(got)
        return got


def add(*terms):
    total = terms[0].astype(jnp.float32)
    for term in terms[1:]:
        total = total + term.astype(jnp.float32)
    return total.astype(jnp.bfloat16)


def with_router(grad_out, routes, probs):
    count, width = grad_out.shape
    chosen = probs.shape[1]
    extra = -(-chosen // 8) * 8
    fill = ((0, extra - chosen), (0, 0))
    routes = jnp.pad(routes.T.astype(jnp.bfloat16), fill, constant_values=-1)
    info = jnp.concatenate([routes, jnp.pad(probs.T, fill)], axis=1)
    return jnp.concatenate([grad_out, jnp.pad(info, ((0, 0), (0, width - 2 * count)))], axis=0)


def gather_local(tokens, grad_out, probs, routes, w_gate, w_up, w_down, gate_pre, up_pre):
    ring = lax.axis_size("seq")
    experts = ring * lax.axis_size("expert")
    count, width = tokens.shape
    chosen = probs.shape[1]
    slot_cap = gate_pre.shape[1] // experts
    seq_place, expert_place = lax.axis_index("seq"), lax.axis_index("expert")
    core_pairs = [(i, i ^ 1) for i in range(4)]
    side_pairs = [(i, i ^ 2) for i in range(4)]
    side, line = Links(2), Links(3)

    def shift(value, by):
        return line.send(value, "seq", [(i, (i + by) % ring) for i in range(ring)])

    def across(value):
        return side.send(value, "expert", side_pairs)

    def other_core(value):
        return lax.ppermute(value, "expert", core_pairs)

    own_expert = expert_place * ring + seq_place

    def ids_of(s):
        place = (seq_place - s) % ring
        return jnp.stack([(expert_place ^ flip) * ring + place for flip in (0, 2, 1, 3)] + [own_expert])

    parts = slopes(gate_pre.reshape(experts, slot_cap, -1), up_pre.reshape(experts, slot_cap, -1))
    rows, dgu, scaled, slots, own, away, sums = {}, {}, {}, {}, {}, {}, {}

    def compute(s):
        pieces = (dy[s], dy_side[s], other_core(dy[s]), other_core(dy_side[s]))
        dx, rows[s], dgu[s], scaled[s], slots[s] = round_backward(
            ids_of(s).astype(jnp.int32), count, pieces, w_down[0], w_gate[0], w_up[0], parts
        )
        own[s] = (dx[0], other_core(dx[2]))
        away[s] = add(dx[1], other_core(dx[3]))

    def give_back(s):
        sums[s] = (*own[s], across(away[s]))
        if s:
            sums[s] = (shift(add(*sums[s]), -s),)

    own_routes = lax.dynamic_slice_in_dim(routes, seq_place * count, count, 0)
    dy, x = {0: with_router(grad_out, own_routes, probs)}, {0: tokens}
    dy_side, x_side = {}, {}
    shifts = sorted(range(ring), key=lambda s: (min(s, ring - s), s))
    for s in shifts[1:]:
        dy[s] = shift(dy[0], s)
    dy_side[0] = across(dy[0])
    x_side[0] = across(x[0])
    done = []
    for s in shifts[1:]:
        dy_side[s] = across(after(dy[s], *done))
        compute(shifts[len(done)])
        done.append(slots[shifts[len(done)]])
    for s in range(1, ring):
        x[s] = shift(x[s - 1], 1)
    for s in shifts:
        if s not in slots:
            compute(s)
        give_back(s)
    for s in range(1, ring):
        x_side[s] = across(x[s])

    back = [term for s in shifts for term in sums[s]]
    total = add(*back)
    pieces = []
    for s in shifts:
        pieces += [x[s], x_side[s], other_core(x[s]), other_core(x_side[s])]
    grads = weight_grads(
        pieces, *[[part[s] for s in shifts] for part in (rows, dgu, scaled, slots)]
    )
    grad_probs = total[count:count + chosen, :count].T
    return (total[:count], grad_probs, *[grad[None] for grad in grads])


def local(tokens, grad_out, probs, routes, w_gate, w_up, w_down, gate_pre, up_pre):
    experts = lax.axis_size("seq") * lax.axis_size("expert")
    gathers = experts * tokens.shape[0] <= 2 * gate_pre.shape[1] and experts <= 256
    plan = gather_local if gathers and lax.axis_size("expert") == 4 else exchange_local
    return plan(tokens, grad_out, probs, routes, w_gate, w_up, w_down, gate_pre, up_pre)


def solution(mesh):
    return jax.shard_map(
        local,
        mesh=mesh,
        in_specs=(
            P(("group", "expert", "seq"), None),
            P(("group", "expert", "seq"), None),
            P(("group", "expert", "seq"), None),
            P(("group", "expert"), None),
            P(("expert", "seq"), None, None),
            P(("expert", "seq"), None, None),
            P(("expert", "seq"), None, None),
            P(("group", "expert", "seq"), None, None),
            P(("group", "expert", "seq"), None, None),
        ),
        out_specs=(
            P(("group", "expert", "seq"), None),
            P(("group", "expert", "seq"), None),
            P(("group", "expert", "seq"), None, None),
            P(("group", "expert", "seq"), None, None),
            P(("group", "expert", "seq"), None, None),
        ),
        check_vma=False,
    )
```

```python
import functools

import jax
import jax.numpy as jnp
from jax import lax
from jax.experimental import pallas as pl
from jax.experimental.pallas import tpu as pltpu
from jax.sharding import PartitionSpec as P


def with_zero(values):
    return jnp.concatenate([values, jnp.zeros((1,) + values.shape[1:], values.dtype)], axis=0)


def block_positions(blocks, experts, slot_cap):
    labels = jnp.arange(experts, dtype=jnp.int32)
    hits = jnp.sum((blocks[..., None] == labels).astype(jnp.int32), axis=-2)
    before = jnp.cumsum(hits, axis=-2) - hits
    ranked = jnp.take_along_axis(before, blocks, axis=-1)
    return blocks * slot_cap + ranked


def invert(places, length):
    entries = places.shape[0]
    return (
        jnp.full((length,), entries, jnp.int32).at[places].set(jnp.arange(entries, dtype=jnp.int32))
    )


def expert_backward(rows_x, rows_dy, rows_p, gate_w, up_w, down_w, gate_in, up_in):
    gate_f = gate_in.astype(jnp.float32)
    up_f = up_in.astype(jnp.float32)
    logistic = jax.nn.sigmoid(gate_f)
    active = gate_f * logistic
    hidden = active * up_f
    back_rows = jnp.dot(rows_dy, down_w.T, preferred_element_type=jnp.float32)
    slot_dprob = jnp.sum(back_rows * hidden, axis=1).astype(jnp.bfloat16)
    weight = rows_p.astype(jnp.float32)[:, None]
    d_hidden = weight * back_rows
    d_up = (d_hidden * active).astype(jnp.bfloat16)
    d_gate = (d_hidden * up_f * logistic * (1.0 + gate_f * (1.0 - logistic))).astype(jnp.bfloat16)
    scaled = (weight * hidden).astype(jnp.bfloat16)
    slot_dx = (
        jnp.dot(d_gate, gate_w.T, preferred_element_type=jnp.float32)
        + jnp.dot(d_up, up_w.T, preferred_element_type=jnp.float32)
    ).astype(jnp.bfloat16)
    grad_gate = jnp.dot(rows_x.T, d_gate, preferred_element_type=jnp.float32).astype(jnp.bfloat16)
    grad_up = jnp.dot(rows_x.T, d_up, preferred_element_type=jnp.float32).astype(jnp.bfloat16)
    grad_down = jnp.dot(scaled.T, rows_dy, preferred_element_type=jnp.float32).astype(jnp.bfloat16)
    return (slot_dx, slot_dprob, grad_gate, grad_up, grad_down)


def exchange_local(tokens, grad_out, probs, routes, w_gate, w_up, w_down, gate_pre, up_pre):
    seq_count = lax.axis_size("seq")
    expert_count = lax.axis_size("expert")
    experts = seq_count * expert_count
    token_count = tokens.shape[0]
    chosen = probs.shape[1]
    width = tokens.shape[1]
    slot_cap = gate_pre.shape[1] // experts
    seq_place = lax.axis_index("seq")
    places = block_positions(routes.reshape(seq_count, token_count, chosen), experts, slot_cap)
    own_places = lax.dynamic_index_in_dim(places, seq_place, 0, keepdims=False)
    lookup = invert(own_places.reshape(-1), experts * slot_cap)
    row_index = lookup // chosen
    send_x = with_zero(tokens)[row_index].reshape(experts, slot_cap, width)
    send_dy = with_zero(grad_out)[row_index].reshape(experts, slot_cap, width)
    send_p = with_zero(probs.reshape(-1))[lookup].reshape(experts, slot_cap)
    got_x, got_dy, got_p = (
        lax.all_to_all(send_x, ("expert", "seq"), split_axis=0, concat_axis=0, tiled=True),
        lax.all_to_all(send_dy, ("expert", "seq"), split_axis=0, concat_axis=0, tiled=True),
        lax.all_to_all(send_p, ("expert", "seq"), split_axis=0, concat_axis=0, tiled=True),
    )
    slot_dx, slot_dprob, grad_gate, grad_up, grad_down = expert_backward(
        got_x.reshape(-1, width),
        got_dy.reshape(-1, width),
        got_p.reshape(-1),
        w_gate[0],
        w_up[0],
        w_down[0],
        gate_pre[0],
        up_pre[0],
    )
    back_x, back_p = (
        lax.all_to_all(
            slot_dx.reshape(experts, slot_cap, width),
            ("expert", "seq"),
            split_axis=0,
            concat_axis=0,
            tiled=True,
        ),
        lax.all_to_all(
            slot_dprob.reshape(experts, slot_cap),
            ("expert", "seq"),
            split_axis=0,
            concat_axis=0,
            tiled=True,
        ),
    )
    flat_x = back_x.reshape(-1, width)
    summed = jnp.zeros((token_count, width), jnp.float32)
    for column in range(chosen):
        summed = summed + flat_x[own_places[:, column]].astype(jnp.float32)
    grad_tokens = summed.astype(jnp.bfloat16)
    grad_probs = back_p.reshape(-1)[own_places]
    return (grad_tokens, grad_probs, grad_gate[None], grad_up[None], grad_down[None])


TILE = 512
STEP = 1024
VMEM = 60 << 20


def dot_nt(a, b):
    return lax.dot_general(a, b, (((1,), (1,)), ((), ())), preferred_element_type=jnp.float32)


def dot_tn(a, b):
    return lax.dot_general(a, b, (((0,), (0,)), ((), ())), preferred_element_type=jnp.float32)


def slot_hits(slots, slot_cap):
    shape = (slot_cap, slots.shape[1])
    return lax.broadcasted_iota(jnp.int32, shape, 0) == jnp.broadcast_to(slots, shape)


def slots_of(named, before):
    taken = jnp.max(jnp.where(named, 1.0, 0.0), axis=0, keepdims=True)
    ranked = jnp.dot(
        jnp.broadcast_to(taken, named.shape).astype(jnp.bfloat16), before, preferred_element_type=jnp.float32
    )
    return jnp.where(taken > 0.0, ranked[:1], -1.0).astype(jnp.int32)


def as_bf16(hits):
    return jnp.where(hits, 1.0, 0.0).astype(jnp.bfloat16)


def slope_kernel(gate_ref, up_ref, out_ref):
    hid = gate_ref.shape[2]
    gate_f = gate_ref[...].astype(jnp.float32)
    up_f = up_ref[...].astype(jnp.float32)
    logistic = jax.nn.sigmoid(gate_f)
    active = gate_f * logistic
    out_ref[:, :, :hid] = up_f * logistic * (1.0 + gate_f * (1.0 - logistic))
    out_ref[:, :, hid:2 * hid] = active
    out_ref[:, :, 2 * hid:] = active * up_f


def slopes(gate_in, up_in):
    blocks, slot_cap, hid = gate_in.shape
    spec = pl.BlockSpec((2, slot_cap, hid), lambda i: (i, 0, 0))
    return pl.pallas_call(
        slope_kernel,
        grid=(blocks // 2,),
        out_shape=jax.ShapeDtypeStruct((blocks, slot_cap, 3 * hid), jnp.float32),
        in_specs=[spec] * 2,
        out_specs=pl.BlockSpec((2, slot_cap, 3 * hid), lambda i: (i, 0, 0)),
        cost_estimate=pl.CostEstimate(
            flops=10 * gate_in.size, bytes_accessed=16 * gate_in.size, transcendentals=gate_in.size
        ),
    )(gate_in, up_in)


def round_kernel(
    ids_ref, dy0, dy1, dy2, dy3, down_hbm, gate_w_hbm, up_w_hbm, slope_hbm,
    dx0, dx1, dx2, dx3, rows_hbm, dgu_hbm, scaled_hbm, slot_ref,
    dy_ref, info_ref, down_ref, both_w_ref, slope_ref,
    dx_ref, extra_ref, rows_ref, dgu_ref, scaled_ref, in_sems, out_sems,
):
    pieces, results = (dy0, dy1, dy2, dy3), (dx0, dx1, dx2, dx3)
    slot_cap, hid = slope_ref.shape[1], scaled_ref.shape[1]
    height, width = dy0.shape
    count = slot_ref.shape[2]
    taken = 4 * slot_cap
    half = width // 2

    started = []

    def fetch(source, target):
        copy = pltpu.make_async_copy(source, target, in_sems.at[len(started)])
        copy.start()
        started.append(copy)
        return copy

    sent = []

    def send(source, target):
        copy = pltpu.make_async_copy(source, target, out_sems.at[len(sent)])
        copy.start()
        sent.append(copy)

    infos = [fetch(pieces[i].at[count:height, :2 * count], info_ref.at[i]) for i in range(4)]
    tiles = []
    for part in range(2):
        cols = slice(part * half, (part + 1) * half)
        tiles.append(
            [fetch(pieces[i].at[:count, cols], dy_ref.at[i * count:(i + 1) * count, cols]) for i in range(4)]
            + [fetch(down_hbm.at[:, cols], down_ref.at[:, cols])]
        )
    ready = [fetch(slope_hbm.at[ids_ref[i]], slope_ref.at[i]) for i in range(4)]
    weights = []
    for part in range(2):
        span = slice(part * half, (part + 1) * half)
        weights.append(
            [fetch(gate_w_hbm.at[span, :], both_w_ref.at[span, :hid]), fetch(up_w_hbm.at[span, :], both_w_ref.at[span, hid:])]
        )

    expert = ids_ref[4].astype(jnp.float32)
    order = [lax.broadcasted_iota(jnp.int32, (count, count), axis) for axis in (0, 1)]
    before = as_bf16(order[0] < order[1])
    hits, named, probs = [], [], []
    for i in range(4):
        infos[i].wait()
        routes = info_ref[i, :, :count].astype(jnp.float32)
        given = info_ref[i, :, count:].astype(jnp.float32)
        named.append(routes == expert)
        probs.append(jnp.sum(jnp.where(named[i], given, 0.0), axis=0, keepdims=True))
        slot = slots_of(named[i], before)
        slot_ref[i] = slot
        hits.append(slot_hits(slot, slot_cap))
    pairs = []
    for i in (0, 2):
        none = jnp.zeros((slot_cap, count), jnp.bfloat16)
        upper = jnp.concatenate([as_bf16(hits[i]), none], axis=1)
        lower = jnp.concatenate([none, as_bf16(hits[i + 1])], axis=1)
        pairs.append(jnp.concatenate([upper, lower], axis=0))

    back = None
    for part in range(2):
        for copy in tiles[part]:
            copy.wait()
        for start in range(part * half, (part + 1) * half, STEP):
            cols = slice(start, start + STEP)
            for i in range(2):
                span = slice(2 * i * slot_cap, (2 * i + 2) * slot_cap)
                rows = jnp.dot(
                    pairs[i], dy_ref[2 * i * count:(2 * i + 2) * count, cols], preferred_element_type=jnp.float32
                )
                rows_ref[span, cols] = rows.astype(jnp.bfloat16)
            part_back = dot_nt(rows_ref[:, cols], down_ref[:, cols])
            back = part_back if back is None else back + part_back
        cols = slice(part * half, (part + 1) * half)
        send(rows_ref.at[:, cols], rows_hbm.at[:, cols])

    for i in range(4):
        ready[i].wait()
        span = slice(i * slot_cap, (i + 1) * slot_cap)
        back_rows = back[span, :]
        hidden = slope_ref[i, :, 2 * hid:]
        weight = jnp.broadcast_to(probs[i], hits[i].shape)
        weight = jnp.sum(jnp.where(hits[i], weight, 0.0), axis=1, keepdims=True)
        dprob = jnp.sum(back_rows * hidden, axis=1, keepdims=True)
        dprob = jnp.broadcast_to(dprob, hits[i].shape)
        dprob = jnp.sum(jnp.where(hits[i], dprob, 0.0), axis=0, keepdims=True)
        dprob = jnp.where(named[i], jnp.broadcast_to(dprob, named[i].shape), 0.0)
        extra_ref[i, :, :count] = dprob.astype(jnp.bfloat16)
        extra_ref[i, :, count:] = jnp.zeros((height - count, width - count), jnp.bfloat16)
        send(extra_ref.at[i], results[i].at[count:height, :])
        d_hidden = weight * back_rows
        dgu_ref[span, :hid] = (d_hidden * slope_ref[i, :, :hid]).astype(jnp.bfloat16)
        dgu_ref[span, hid:] = (d_hidden * slope_ref[i, :, hid:2 * hid]).astype(jnp.bfloat16)
        scaled_ref[span, :] = (weight * hidden).astype(jnp.bfloat16)
    send(dgu_ref, dgu_hbm)
    send(scaled_ref, scaled_hbm)

    for part in range(2):
        for copy in weights[part]:
            copy.wait()
        for start in range(part * half, (part + 1) * half, STEP):
            cols = slice(start, start + STEP)
            slot_dx = dot_nt(dgu_ref[...], both_w_ref[cols, :]).astype(jnp.bfloat16)
            for i in range(2):
                span = slice(2 * i * slot_cap, (2 * i + 2) * slot_cap)
                both = dot_tn(pairs[i], slot_dx[span, :]).astype(jnp.bfloat16)
                dx_ref[2 * i * count:(2 * i + 2) * count, cols] = both
        cols = slice(part * half, (part + 1) * half)
        for i in (2, 3, 1, 0):
            send(dx_ref.at[i * count:(i + 1) * count, cols], results[i].at[:count, cols])
    for copy in sent:
        copy.wait()


def round_backward(ids, count, pieces, down_w, gate_w, up_w, parts):
    height, width = pieces[0].shape
    slot_cap, hid = parts.shape[1], parts.shape[2] // 3
    taken = 4 * slot_cap
    half = jnp.bfloat16
    anywhere = pl.BlockSpec(memory_space=pl.ANY)
    flops = 2 * taken * width * (3 * hid + 2 * count)
    moved = 2 * (3 * width * hid + 8 * height * width + taken * (width + 5 * hid))
    out = pl.pallas_call(
        round_kernel,
        out_shape=[jax.ShapeDtypeStruct((height, width), half)] * 4
        + [
            jax.ShapeDtypeStruct((taken, width), half),
            jax.ShapeDtypeStruct((taken, 2 * hid), half),
            jax.ShapeDtypeStruct((taken, hid), half),
            jax.ShapeDtypeStruct((4, 1, count), jnp.int32),
        ],
        in_specs=[pl.BlockSpec(memory_space=pltpu.SMEM)] + [anywhere] * 8,
        out_specs=[anywhere] * 7 + [pl.BlockSpec(memory_space=pltpu.VMEM)],
        scratch_shapes=[
            pltpu.VMEM((4 * count, width), half),
            pltpu.VMEM((4, height - count, 2 * count), half),
            pltpu.VMEM(down_w.shape, half),
            pltpu.VMEM((width, 2 * hid), half),
            pltpu.VMEM((4, slot_cap, 3 * hid), jnp.float32),
            pltpu.VMEM((4 * count, width), half),
            pltpu.VMEM((4, height - count, width), half),
            pltpu.VMEM((taken, width), half),
            pltpu.VMEM((taken, 2 * hid), half),
            pltpu.VMEM((taken, hid), half),
            pltpu.SemaphoreType.DMA((22,)),
            pltpu.SemaphoreType.DMA((16,)),
        ],
        compiler_params=pltpu.CompilerParams(vmem_limit_bytes=VMEM),
        cost_estimate=pl.CostEstimate(flops=flops, bytes_accessed=moved, transcendentals=0),
    )(ids, *pieces, down_w, gate_w, up_w, parts)
    return out[:4], out[4], out[5], out[6], out[7]


def columns(height):
    return pl.BlockSpec((height, TILE), lambda i: (0, i))


def whole(array):
    return pl.BlockSpec(array.shape, lambda i: (0,) * array.ndim)


def down_kernel(rounds, *refs):
    scaled, rows = refs[:rounds], refs[rounds:2 * rounds]
    out, all_scaled, all_dy = refs[2 * rounds:]
    taken = rows[0].shape[0]

    @pl.when(pl.program_id(0) == 0)
    def _():
        for r in range(rounds):
            all_scaled[r * taken:(r + 1) * taken, :] = scaled[r][...]

    for r in range(rounds):
        all_dy[r * taken:(r + 1) * taken, :] = rows[r][...]
    out[...] = dot_tn(all_scaled[...], all_dy[...]).astype(jnp.bfloat16)


def down_grad(scaled, rows):
    rounds = len(rows)
    taken, hid = scaled[0].shape
    width = rows[0].shape[1]
    total = rounds * taken
    return pl.pallas_call(
        functools.partial(down_kernel, rounds),
        grid=(width // TILE,),
        out_shape=jax.ShapeDtypeStruct((hid, width), jnp.bfloat16),
        in_specs=[whole(part) for part in scaled] + [columns(taken)] * rounds,
        out_specs=columns(hid),
        scratch_shapes=[pltpu.VMEM((total, hid), jnp.bfloat16), pltpu.VMEM((total, TILE), jnp.bfloat16)],
        compiler_params=pltpu.CompilerParams(vmem_limit_bytes=VMEM),
        cost_estimate=pl.CostEstimate(
            flops=2 * total * width * hid, bytes_accessed=2 * (total * (width + hid) + width * hid), transcendentals=0
        ),
    )(*scaled, *rows)


def input_kernel(rounds, slot_cap, halved, *refs):
    count = 4 * rounds
    pieces, refs = [], list(refs)
    left = pl.program_id(0) < pl.num_programs(0) // 2
    for split in halved:
        piece = refs.pop(0)[...]
        pieces.append(jnp.where(left, piece, refs.pop(0)[...]) if split else piece)
    dgu, slots = refs[:rounds], refs[rounds:2 * rounds]
    gate_out, up_out, all_x, all_dgu = refs[2 * rounds:]
    taken = 4 * slot_cap
    hid = gate_out.shape[1]

    @pl.when(pl.program_id(0) == 0)
    def _():
        for r in range(rounds):
            all_dgu[r * taken:(r + 1) * taken, :] = dgu[r][...]

    for i in range(count):
        select = as_bf16(slot_hits(slots[i // 4][i % 4], slot_cap))
        picked = jnp.dot(select, pieces[i], preferred_element_type=jnp.float32)
        all_x[i * slot_cap:(i + 1) * slot_cap, :] = picked.astype(jnp.bfloat16)
    grads = dot_tn(all_x[...], all_dgu[...])
    gate_out[...] = grads[:, :hid].astype(jnp.bfloat16)
    up_out[...] = grads[:, hid:].astype(jnp.bfloat16)


def input_grads(width, pieces, dgu, slots):
    rounds, count = len(dgu), len(pieces)
    taken, both = dgu[0].shape
    hid = both // 2
    half = jnp.bfloat16
    steps = width // TILE
    halved = tuple(isinstance(piece, tuple) for piece in pieces)
    flat, specs = [], []
    for piece, split in zip(pieces, halved, strict=True):
        flat += piece if split else (piece,)
        size = flat[-1].shape[0]
        if split:
            last = flat[-1].shape[1] // TILE - steps
            specs.append(pl.BlockSpec((size, TILE), lambda i: (0, jnp.minimum(i, steps // 2 - 1))))
            specs.append(pl.BlockSpec((size, TILE), lambda i, last=last: (0, jnp.maximum(i, steps // 2) + last)))
        else:
            specs.append(columns(size))
    slot_cap, total = taken // 4, rounds * taken
    flops = 2 * total * width * (2 * hid + size)
    moved = 2 * (count * size * width + total * 2 * hid + 2 * width * hid)
    strip = pl.BlockSpec((TILE, hid), lambda i: (i, 0))
    return pl.pallas_call(
        functools.partial(input_kernel, rounds, slot_cap, halved),
        grid=(steps,),
        out_shape=[jax.ShapeDtypeStruct((width, hid), half)] * 2,
        in_specs=specs + [whole(part) for part in dgu] + [whole(part) for part in slots],
        out_specs=[strip] * 2,
        scratch_shapes=[pltpu.VMEM((total, TILE), half), pltpu.VMEM((total, both), half)],
        compiler_params=pltpu.CompilerParams(vmem_limit_bytes=VMEM),
        cost_estimate=pl.CostEstimate(flops=flops, bytes_accessed=moved, transcendentals=0),
    )(*flat, *dgu, *slots)


def after(value, *others):
    return value if not others else lax.optimization_barrier((value, *others))[0]


class Links:
    def __init__(self, depth):
        self.depth, self.arrived = depth, []

    def send(self, value, axis, pairs):
        if len(self.arrived) >= self.depth:
            value = after(value, self.arrived[-self.depth])
        got = lax.ppermute(value, axis, pairs)
        self.arrived.append(got)
        return got


def add(*terms):
    total = terms[0].astype(jnp.float32)
    for term in terms[1:]:
        total = total + term.astype(jnp.float32)
    return total.astype(jnp.bfloat16)


def with_router(grad_out, routes, probs):
    count, width = grad_out.shape
    chosen = probs.shape[1]
    extra = -(-chosen // 8) * 8
    fill = ((0, extra - chosen), (0, 0))
    routes = jnp.pad(routes.T.astype(jnp.bfloat16), fill, constant_values=-1)
    info = jnp.concatenate([routes, jnp.pad(probs.T, fill)], axis=1)
    return jnp.concatenate([grad_out, jnp.pad(info, ((0, 0), (0, width - 2 * count)))], axis=0)


def gather_local(tokens, grad_out, probs, routes, w_gate, w_up, w_down, gate_pre, up_pre):
    ring = lax.axis_size("seq")
    experts = ring * lax.axis_size("expert")
    count, width = tokens.shape
    chosen = probs.shape[1]
    slot_cap = gate_pre.shape[1] // experts
    seq_place, expert_place = lax.axis_index("seq"), lax.axis_index("expert")
    core_pairs = [(i, i ^ 1) for i in range(4)]
    side_pairs = [(i, i ^ 2) for i in range(4)]
    side, line = Links(2), Links(3)

    def shift(value, by):
        return line.send(value, "seq", [(i, (i + by) % ring) for i in range(ring)])

    def across(value):
        return side.send(value, "expert", side_pairs)

    def other_core(value):
        return lax.ppermute(value, "expert", core_pairs)

    own_expert = expert_place * ring + seq_place

    def ids_of(s):
        place = (seq_place - s) % ring
        return jnp.stack([(expert_place ^ flip) * ring + place for flip in (0, 2, 1, 3)] + [own_expert])

    parts = slopes(gate_pre.reshape(experts, slot_cap, -1), up_pre.reshape(experts, slot_cap, -1))
    rows, dgu, scaled, slots, own, away, sums = {}, {}, {}, {}, {}, {}, {}

    def compute(s):
        pieces = (dy[s], dy_side[s], other_core(dy[s]), other_core(dy_side[s]))
        dx, rows[s], dgu[s], scaled[s], slots[s] = round_backward(
            ids_of(s).astype(jnp.int32), count, pieces, w_down[0], w_gate[0], w_up[0], parts
        )
        own[s] = (dx[0], other_core(dx[2]))
        away[s] = add(dx[1], other_core(dx[3]))

    def give_back(s):
        sums[s] = (*own[s], across(away[s]))
        if s:
            sums[s] = (shift(add(*sums[s]), -s),)

    own_routes = lax.dynamic_slice_in_dim(routes, seq_place * count, count, 0)
    dy, x = {0: with_router(grad_out, own_routes, probs)}, {0: tokens}
    dy_side, x_side = {}, {}
    shifts = sorted(range(ring), key=lambda s: (min(s, ring - s), s))
    for s in shifts[1:]:
        dy[s] = shift(dy[0], s)
    dy_side[0] = across(dy[0])
    x_side[0] = across(x[0])
    done = []
    for s in shifts[1:]:
        dy_side[s] = across(after(dy[s], *done))
        compute(shifts[len(done)])
        done.append(slots[shifts[len(done)]])
    for s in range(1, ring):
        x[s] = shift(x[s - 1], 1)
    for s in shifts:
        if s not in slots:
            compute(s)
        give_back(s)
    for s in range(1, ring):
        x_side[s] = across(x[s])

    back = [term for s in shifts for term in sums[s]]
    total = add(*back)
    pieces = {0: [tokens, x_side[0], other_core(tokens), other_core(x_side[0])]}
    for s in range(1, ring):
        held, side_held = other_core(x[s]), other_core(x_side[s])
        pieces[s] = [x[s], x_side[s], held, side_held]
    first = after(rows[shifts[0]], *[slots[s] for s in shifts])
    grad_down = down_grad([scaled[s] for s in shifts], [first] + [rows[s] for s in shifts[1:]])
    grad_gate, grad_up = input_grads(
        width,
        [piece for s in shifts for piece in pieces[s]], *[[part[s] for s in shifts] for part in (dgu, slots)]
    )
    grad_probs = total[count:count + chosen, :count].T
    return (total[:count], grad_probs, grad_gate[None], grad_up[None], grad_down[None])


def local(tokens, grad_out, probs, routes, w_gate, w_up, w_down, gate_pre, up_pre):
    experts = lax.axis_size("seq") * lax.axis_size("expert")
    gathers = experts * tokens.shape[0] <= 2 * gate_pre.shape[1] and experts <= 256
    plan = gather_local if gathers and lax.axis_size("expert") == 4 else exchange_local
    return plan(tokens, grad_out, probs, routes, w_gate, w_up, w_down, gate_pre, up_pre)


def solution(mesh):
    return jax.shard_map(
        local,
        mesh=mesh,
        in_specs=(
            P(("group", "expert", "seq"), None),
            P(("group", "expert", "seq"), None),
            P(("group", "expert", "seq"), None),
            P(("group", "expert"), None),
            P(("expert", "seq"), None, None),
            P(("expert", "seq"), None, None),
            P(("expert", "seq"), None, None),
            P(("group", "expert", "seq"), None, None),
            P(("group", "expert", "seq"), None, None),
        ),
        out_specs=(
            P(("group", "expert", "seq"), None),
            P(("group", "expert", "seq"), None),
            P(("group", "expert", "seq"), None, None),
            P(("group", "expert", "seq"), None, None),
            P(("group", "expert", "seq"), None, None),
        ),
        check_vma=False,
    )
```

```python
import functools
import math

import jax
import jax.numpy as jnp
from jax import lax
from jax.experimental import pallas as pl
from jax.experimental.pallas import tpu as pltpu
from jax.sharding import PartitionSpec as P


def with_zero(values):
    return jnp.concatenate([values, jnp.zeros((1,) + values.shape[1:], values.dtype)], axis=0)


def block_positions(blocks, experts, slot_cap):
    labels = jnp.arange(experts, dtype=jnp.int32)
    hits = jnp.sum((blocks[..., None] == labels).astype(jnp.int32), axis=-2)
    before = jnp.cumsum(hits, axis=-2) - hits
    ranked = jnp.take_along_axis(before, blocks, axis=-1)
    return blocks * slot_cap + ranked


def invert(places, length):
    entries = places.shape[0]
    return (
        jnp.full((length,), entries, jnp.int32).at[places].set(jnp.arange(entries, dtype=jnp.int32))
    )


def expert_backward(rows_x, rows_dy, rows_p, gate_w, up_w, down_w, gate_in, up_in):
    gate_f = gate_in.astype(jnp.float32)
    up_f = up_in.astype(jnp.float32)
    logistic = jax.nn.sigmoid(gate_f)
    active = gate_f * logistic
    hidden = active * up_f
    back_rows = jnp.dot(rows_dy, down_w.T, preferred_element_type=jnp.float32)
    slot_dprob = jnp.sum(back_rows * hidden, axis=1).astype(jnp.bfloat16)
    weight = rows_p.astype(jnp.float32)[:, None]
    d_hidden = weight * back_rows
    d_up = (d_hidden * active).astype(jnp.bfloat16)
    d_gate = (d_hidden * up_f * logistic * (1.0 + gate_f * (1.0 - logistic))).astype(jnp.bfloat16)
    scaled = (weight * hidden).astype(jnp.bfloat16)
    slot_dx = (
        jnp.dot(d_gate, gate_w.T, preferred_element_type=jnp.float32)
        + jnp.dot(d_up, up_w.T, preferred_element_type=jnp.float32)
    ).astype(jnp.bfloat16)
    grad_gate = jnp.dot(rows_x.T, d_gate, preferred_element_type=jnp.float32).astype(jnp.bfloat16)
    grad_up = jnp.dot(rows_x.T, d_up, preferred_element_type=jnp.float32).astype(jnp.bfloat16)
    grad_down = jnp.dot(scaled.T, rows_dy, preferred_element_type=jnp.float32).astype(jnp.bfloat16)
    return (slot_dx, slot_dprob, grad_gate, grad_up, grad_down)


def exchange_local(tokens, grad_out, probs, routes, w_gate, w_up, w_down, gate_pre, up_pre):
    seq_count = lax.axis_size("seq")
    expert_count = lax.axis_size("expert")
    experts = seq_count * expert_count
    token_count = tokens.shape[0]
    chosen = probs.shape[1]
    width = tokens.shape[1]
    slot_cap = gate_pre.shape[1] // experts
    seq_place = lax.axis_index("seq")
    places = block_positions(routes.reshape(seq_count, token_count, chosen), experts, slot_cap)
    own_places = lax.dynamic_index_in_dim(places, seq_place, 0, keepdims=False)
    lookup = invert(own_places.reshape(-1), experts * slot_cap)
    row_index = lookup // chosen
    send_x = with_zero(tokens)[row_index].reshape(experts, slot_cap, width)
    send_dy = with_zero(grad_out)[row_index].reshape(experts, slot_cap, width)
    send_p = with_zero(probs.reshape(-1))[lookup].reshape(experts, slot_cap)
    got_x, got_dy, got_p = (
        lax.all_to_all(send_x, ("expert", "seq"), split_axis=0, concat_axis=0, tiled=True),
        lax.all_to_all(send_dy, ("expert", "seq"), split_axis=0, concat_axis=0, tiled=True),
        lax.all_to_all(send_p, ("expert", "seq"), split_axis=0, concat_axis=0, tiled=True),
    )
    slot_dx, slot_dprob, grad_gate, grad_up, grad_down = expert_backward(
        got_x.reshape(-1, width),
        got_dy.reshape(-1, width),
        got_p.reshape(-1),
        w_gate[0],
        w_up[0],
        w_down[0],
        gate_pre[0],
        up_pre[0],
    )
    back_x, back_p = (
        lax.all_to_all(
            slot_dx.reshape(experts, slot_cap, width),
            ("expert", "seq"),
            split_axis=0,
            concat_axis=0,
            tiled=True,
        ),
        lax.all_to_all(
            slot_dprob.reshape(experts, slot_cap),
            ("expert", "seq"),
            split_axis=0,
            concat_axis=0,
            tiled=True,
        ),
    )
    flat_x = back_x.reshape(-1, width)
    summed = jnp.zeros((token_count, width), jnp.float32)
    for column in range(chosen):
        summed = summed + flat_x[own_places[:, column]].astype(jnp.float32)
    grad_tokens = summed.astype(jnp.bfloat16)
    grad_probs = back_p.reshape(-1)[own_places]
    return (grad_tokens, grad_probs, grad_gate[None], grad_up[None], grad_down[None])


TILE = 512
STEP = 1024
VMEM = 60 << 20


def dot_nt(a, b):
    return lax.dot_general(a, b, (((1,), (1,)), ((), ())), preferred_element_type=jnp.float32)


def dot_tn(a, b):
    return lax.dot_general(a, b, (((0,), (0,)), ((), ())), preferred_element_type=jnp.float32)


def slot_hits(slots, slot_cap):
    shape = (slot_cap, slots.shape[1])
    return lax.broadcasted_iota(jnp.int32, shape, 0) == jnp.broadcast_to(slots, shape)


def slots_of(named, before):
    taken = jnp.max(jnp.where(named, 1.0, 0.0), axis=0, keepdims=True)
    ranked = jnp.dot(
        jnp.broadcast_to(taken, named.shape).astype(jnp.bfloat16), before, preferred_element_type=jnp.float32
    )
    return jnp.where(taken > 0.0, ranked[:1], -1.0).astype(jnp.int32)


def as_bf16(hits):
    return jnp.where(hits, 1.0, 0.0).astype(jnp.bfloat16)


def slope_kernel(gate_ref, up_ref, out_ref):
    hid = gate_ref.shape[2]
    gate_f = gate_ref[...].astype(jnp.float32)
    up_f = up_ref[...].astype(jnp.float32)
    logistic = jax.nn.sigmoid(gate_f)
    active = gate_f * logistic
    out_ref[:, :, :hid] = up_f * logistic * (1.0 + gate_f * (1.0 - logistic))
    out_ref[:, :, hid:2 * hid] = active
    out_ref[:, :, 2 * hid:] = active * up_f


def slopes(gate_in, up_in):
    blocks, slot_cap, hid = gate_in.shape
    step = math.gcd(blocks, 4)
    spec = pl.BlockSpec((step, slot_cap, hid), lambda i: (i, 0, 0))
    return pl.pallas_call(
        slope_kernel,
        grid=(blocks // step,),
        out_shape=jax.ShapeDtypeStruct((blocks, slot_cap, 3 * hid), jnp.float32),
        in_specs=[spec] * 2,
        out_specs=pl.BlockSpec((step, slot_cap, 3 * hid), lambda i: (i, 0, 0)),
        cost_estimate=pl.CostEstimate(
            flops=10 * gate_in.size, bytes_accessed=16 * gate_in.size, transcendentals=gate_in.size
        ),
    )(gate_in, up_in)


def round_kernel(
    ids_ref, dy0, dy1, dy2, dy3, down_hbm, gate_w_hbm, up_w_hbm, slope_hbm,
    dx0, dx1, dx2, dx3, rows_hbm, dgu_hbm, scaled_hbm, slot_ref,
    dy_ref, info_ref, down_ref, both_w_ref, slope_ref,
    dx_ref, extra_ref, rows_ref, dgu_ref, scaled_ref, in_sems, out_sems,
):
    pieces, results = (dy0, dy1, dy2, dy3), (dx0, dx1, dx2, dx3)
    slot_cap, hid = slope_ref.shape[1], scaled_ref.shape[1]
    height, width = dy0.shape
    count = slot_ref.shape[2]
    taken = 4 * slot_cap
    half = width // 2

    started = []

    def fetch(source, target):
        copy = pltpu.make_async_copy(source, target, in_sems.at[len(started)])
        copy.start()
        started.append(copy)
        return copy

    sent = []

    def send(source, target):
        copy = pltpu.make_async_copy(source, target, out_sems.at[len(sent)])
        copy.start()
        sent.append(copy)

    infos = [fetch(pieces[i].at[count:height, :2 * count], info_ref.at[i]) for i in range(4)]
    tiles = []
    for part in range(2):
        cols = slice(part * half, (part + 1) * half)
        tiles.append(
            [fetch(pieces[i].at[:count, cols], dy_ref.at[i * count:(i + 1) * count, cols]) for i in range(4)]
            + [fetch(down_hbm.at[:, cols], down_ref.at[:, cols])]
        )
    ready = [fetch(slope_hbm.at[ids_ref[i]], slope_ref.at[i]) for i in range(4)]
    weights = []
    for part in range(2):
        span = slice(part * half, (part + 1) * half)
        weights.append(
            [fetch(gate_w_hbm.at[span, :], both_w_ref.at[span, :hid]), fetch(up_w_hbm.at[span, :], both_w_ref.at[span, hid:])]
        )

    expert = ids_ref[4].astype(jnp.float32)
    order = [lax.broadcasted_iota(jnp.int32, (count, count), axis) for axis in (0, 1)]
    before = as_bf16(order[0] < order[1])
    hits, named, probs = [], [], []
    for i in range(4):
        infos[i].wait()
        routes = info_ref[i, :, :count].astype(jnp.float32)
        given = info_ref[i, :, count:].astype(jnp.float32)
        named.append(routes == expert)
        probs.append(jnp.sum(jnp.where(named[i], given, 0.0), axis=0, keepdims=True))
        slot = slots_of(named[i], before)
        slot_ref[i] = slot
        hits.append(slot_hits(slot, slot_cap))
    pairs = []
    for i in (0, 2):
        none = jnp.zeros((slot_cap, count), jnp.bfloat16)
        upper = jnp.concatenate([as_bf16(hits[i]), none], axis=1)
        lower = jnp.concatenate([none, as_bf16(hits[i + 1])], axis=1)
        pairs.append(jnp.concatenate([upper, lower], axis=0))

    back = None
    for part in range(2):
        for copy in tiles[part]:
            copy.wait()
        for start in range(part * half, (part + 1) * half, STEP):
            cols = slice(start, start + STEP)
            for i in range(2):
                span = slice(2 * i * slot_cap, (2 * i + 2) * slot_cap)
                rows = jnp.dot(
                    pairs[i], dy_ref[2 * i * count:(2 * i + 2) * count, cols], preferred_element_type=jnp.float32
                )
                rows_ref[span, cols] = rows.astype(jnp.bfloat16)
            part_back = dot_nt(rows_ref[:, cols], down_ref[:, cols])
            back = part_back if back is None else back + part_back
        cols = slice(part * half, (part + 1) * half)
        send(rows_ref.at[:, cols], rows_hbm.at[:, cols])

    for i in range(4):
        ready[i].wait()
        span = slice(i * slot_cap, (i + 1) * slot_cap)
        back_rows = back[span, :]
        hidden = slope_ref[i, :, 2 * hid:]
        weight = jnp.broadcast_to(probs[i], hits[i].shape)
        weight = jnp.sum(jnp.where(hits[i], weight, 0.0), axis=1, keepdims=True)
        dprob = jnp.sum(back_rows * hidden, axis=1, keepdims=True)
        dprob = jnp.broadcast_to(dprob, hits[i].shape)
        dprob = jnp.sum(jnp.where(hits[i], dprob, 0.0), axis=0, keepdims=True)
        dprob = jnp.where(named[i], jnp.broadcast_to(dprob, named[i].shape), 0.0)
        extra_ref[i, :, :count] = dprob.astype(jnp.bfloat16)
        extra_ref[i, :, count:] = jnp.zeros((height - count, width - count), jnp.bfloat16)
        send(extra_ref.at[i], results[i].at[count:height, :])
        d_hidden = weight * back_rows
        dgu_ref[span, :hid] = (d_hidden * slope_ref[i, :, :hid]).astype(jnp.bfloat16)
        dgu_ref[span, hid:] = (d_hidden * slope_ref[i, :, hid:2 * hid]).astype(jnp.bfloat16)
        scaled_ref[span, :] = (weight * hidden).astype(jnp.bfloat16)
    send(dgu_ref, dgu_hbm)
    send(scaled_ref, scaled_hbm)

    for part in range(2):
        for copy in weights[part]:
            copy.wait()
        for start in range(part * half, (part + 1) * half, STEP):
            cols = slice(start, start + STEP)
            slot_dx = dot_nt(dgu_ref[...], both_w_ref[cols, :]).astype(jnp.bfloat16)
            for i in range(2):
                span = slice(2 * i * slot_cap, (2 * i + 2) * slot_cap)
                both = dot_tn(pairs[i], slot_dx[span, :]).astype(jnp.bfloat16)
                dx_ref[2 * i * count:(2 * i + 2) * count, cols] = both
        cols = slice(part * half, (part + 1) * half)
        for i in (2, 3, 1, 0):
            send(dx_ref.at[i * count:(i + 1) * count, cols], results[i].at[:count, cols])
    for copy in sent:
        copy.wait()


def round_backward(ids, count, pieces, down_w, gate_w, up_w, parts):
    height, width = pieces[0].shape
    slot_cap, hid = parts.shape[1], parts.shape[2] // 3
    taken = 4 * slot_cap
    half = jnp.bfloat16
    anywhere = pl.BlockSpec(memory_space=pl.ANY)
    flops = 2 * taken * width * (3 * hid + 2 * count)
    moved = 2 * (3 * width * hid + 8 * height * width + taken * (width + 5 * hid))
    out = pl.pallas_call(
        round_kernel,
        out_shape=[jax.ShapeDtypeStruct((height, width), half)] * 4
        + [
            jax.ShapeDtypeStruct((taken, width), half),
            jax.ShapeDtypeStruct((taken, 2 * hid), half),
            jax.ShapeDtypeStruct((taken, hid), half),
            jax.ShapeDtypeStruct((4, 1, count), jnp.int32),
        ],
        in_specs=[pl.BlockSpec(memory_space=pltpu.SMEM)] + [anywhere] * 8,
        out_specs=[anywhere] * 7 + [pl.BlockSpec(memory_space=pltpu.VMEM)],
        scratch_shapes=[
            pltpu.VMEM((4 * count, width), half),
            pltpu.VMEM((4, height - count, 2 * count), half),
            pltpu.VMEM(down_w.shape, half),
            pltpu.VMEM((width, 2 * hid), half),
            pltpu.VMEM((4, slot_cap, 3 * hid), jnp.float32),
            pltpu.VMEM((4 * count, width), half),
            pltpu.VMEM((4, height - count, width), half),
            pltpu.VMEM((taken, width), half),
            pltpu.VMEM((taken, 2 * hid), half),
            pltpu.VMEM((taken, hid), half),
            pltpu.SemaphoreType.DMA((22,)),
            pltpu.SemaphoreType.DMA((16,)),
        ],
        compiler_params=pltpu.CompilerParams(vmem_limit_bytes=VMEM),
        cost_estimate=pl.CostEstimate(flops=flops, bytes_accessed=moved, transcendentals=0),
    )(ids, *pieces, down_w, gate_w, up_w, parts)
    return out[:4], out[4], out[5], out[6], out[7]


def columns(height):
    return pl.BlockSpec((height, TILE), lambda i: (0, i))


def whole(array):
    return pl.BlockSpec(array.shape, lambda i: (0,) * array.ndim)


def down_kernel(rounds, *refs):
    scaled, rows = refs[:rounds], refs[rounds:2 * rounds]
    out, all_scaled, all_dy = refs[2 * rounds:]
    taken = rows[0].shape[0]

    @pl.when(pl.program_id(0) == 0)
    def _():
        for r in range(rounds):
            all_scaled[r * taken:(r + 1) * taken, :] = scaled[r][...]

    for r in range(rounds):
        all_dy[r * taken:(r + 1) * taken, :] = rows[r][...]
    out[...] = dot_tn(all_scaled[...], all_dy[...]).astype(jnp.bfloat16)


def down_grad(scaled, rows):
    rounds = len(rows)
    taken, hid = scaled[0].shape
    width = rows[0].shape[1]
    total = rounds * taken
    return pl.pallas_call(
        functools.partial(down_kernel, rounds),
        grid=(width // TILE,),
        out_shape=jax.ShapeDtypeStruct((hid, width), jnp.bfloat16),
        in_specs=[whole(part) for part in scaled] + [columns(taken)] * rounds,
        out_specs=columns(hid),
        scratch_shapes=[pltpu.VMEM((total, hid), jnp.bfloat16), pltpu.VMEM((total, TILE), jnp.bfloat16)],
        compiler_params=pltpu.CompilerParams(vmem_limit_bytes=VMEM),
        cost_estimate=pl.CostEstimate(
            flops=2 * total * width * hid, bytes_accessed=2 * (total * (width + hid) + width * hid), transcendentals=0
        ),
    )(*scaled, *rows)


def input_kernel(rounds, slot_cap, halved, *refs):
    count = 4 * rounds
    pieces, refs = [], list(refs)
    left = pl.program_id(0) < pl.num_programs(0) // 2
    for split in halved:
        piece = refs.pop(0)[...]
        pieces.append(jnp.where(left, piece, refs.pop(0)[...]) if split else piece)
    dgu, slots = refs[:rounds], refs[rounds:2 * rounds]
    gate_out, up_out, all_x, all_dgu = refs[2 * rounds:]
    taken = 4 * slot_cap
    hid = gate_out.shape[1]

    @pl.when(pl.program_id(0) == 0)
    def _():
        for r in range(rounds):
            all_dgu[r * taken:(r + 1) * taken, :] = dgu[r][...]

    for i in range(count):
        select = as_bf16(slot_hits(slots[i // 4][i % 4], slot_cap))
        picked = jnp.dot(select, pieces[i], preferred_element_type=jnp.float32)
        all_x[i * slot_cap:(i + 1) * slot_cap, :] = picked.astype(jnp.bfloat16)
    grads = dot_tn(all_x[...], all_dgu[...])
    gate_out[...] = grads[:, :hid].astype(jnp.bfloat16)
    up_out[...] = grads[:, hid:].astype(jnp.bfloat16)


def input_grads(width, pieces, dgu, slots):
    rounds, count = len(dgu), len(pieces)
    taken, both = dgu[0].shape
    hid = both // 2
    half = jnp.bfloat16
    steps = width // TILE
    halved = tuple(isinstance(piece, tuple) for piece in pieces)
    flat, specs = [], []
    for piece, split in zip(pieces, halved, strict=True):
        flat += piece if split else (piece,)
        size = flat[-1].shape[0]
        if split:
            last = flat[-1].shape[1] // TILE - steps
            specs.append(pl.BlockSpec((size, TILE), lambda i: (0, jnp.minimum(i, steps // 2 - 1))))
            specs.append(pl.BlockSpec((size, TILE), lambda i, last=last: (0, jnp.maximum(i, steps // 2) + last)))
        else:
            specs.append(columns(size))
    slot_cap, total = taken // 4, rounds * taken
    flops = 2 * total * width * (2 * hid + size)
    moved = 2 * (count * size * width + total * 2 * hid + 2 * width * hid)
    strip = pl.BlockSpec((TILE, hid), lambda i: (i, 0))
    return pl.pallas_call(
        functools.partial(input_kernel, rounds, slot_cap, halved),
        grid=(steps,),
        out_shape=[jax.ShapeDtypeStruct((width, hid), half)] * 2,
        in_specs=specs + [whole(part) for part in dgu] + [whole(part) for part in slots],
        out_specs=[strip] * 2,
        scratch_shapes=[pltpu.VMEM((total, TILE), half), pltpu.VMEM((total, both), half)],
        compiler_params=pltpu.CompilerParams(vmem_limit_bytes=VMEM),
        cost_estimate=pl.CostEstimate(flops=flops, bytes_accessed=moved, transcendentals=0),
    )(*flat, *dgu, *slots)


def after(value, *others):
    return value if not others else lax.optimization_barrier((value, *others))[0]


class Links:
    def __init__(self, depth):
        self.depth, self.arrived = depth, []

    def send(self, value, axis, pairs):
        if len(self.arrived) >= self.depth:
            value = after(value, self.arrived[-self.depth])
        got = lax.ppermute(value, axis, pairs)
        self.arrived.append(got)
        return got


def add(*terms):
    total = terms[0].astype(jnp.float32)
    for term in terms[1:]:
        total = total + term.astype(jnp.float32)
    return total.astype(jnp.bfloat16)


def with_router(grad_out, routes, probs):
    count, width = grad_out.shape
    chosen = probs.shape[1]
    extra = -(-chosen // 8) * 8
    fill = ((0, extra - chosen), (0, 0))
    routes = jnp.pad(routes.T.astype(jnp.bfloat16), fill, constant_values=-1)
    info = jnp.concatenate([routes, jnp.pad(probs.T, fill)], axis=1)
    return jnp.concatenate([grad_out, jnp.pad(info, ((0, 0), (0, width - 2 * count)))], axis=0)


def gather_local(tokens, grad_out, probs, routes, w_gate, w_up, w_down, gate_pre, up_pre):
    ring = lax.axis_size("seq")
    experts = ring * lax.axis_size("expert")
    count, width = tokens.shape
    chosen = probs.shape[1]
    slot_cap = gate_pre.shape[1] // experts
    seq_place, expert_place = lax.axis_index("seq"), lax.axis_index("expert")
    core_pairs = [(i, i ^ 1) for i in range(4)]
    side_pairs = [(i, i ^ 2) for i in range(4)]
    side, line = Links(2), Links(3)

    def shift(value, by):
        return line.send(value, "seq", [(i, (i + by) % ring) for i in range(ring)])

    def across(value):
        return side.send(value, "expert", side_pairs)

    def other_core(value):
        return lax.ppermute(value, "expert", core_pairs)

    own_expert = expert_place * ring + seq_place

    def ids_of(s):
        place = (seq_place - s) % ring
        return jnp.stack([(expert_place ^ flip) * ring + place for flip in (0, 2, 1, 3)] + [own_expert])

    parts = slopes(gate_pre.reshape(experts, slot_cap, -1), up_pre.reshape(experts, slot_cap, -1))
    rows, dgu, scaled, slots, own, away, sums = {}, {}, {}, {}, {}, {}, {}

    def compute(s):
        pieces = (dy[s], dy_side[s], other_core(dy[s]), other_core(dy_side[s]))
        dx, rows[s], dgu[s], scaled[s], slots[s] = round_backward(
            ids_of(s).astype(jnp.int32), count, pieces, w_down[0], w_gate[0], w_up[0], parts
        )
        own[s] = (dx[0], other_core(dx[2]))
        away[s] = add(dx[1], other_core(dx[3]))

    def give_back(s):
        sums[s] = (*own[s], across(away[s]))
        if s:
            sums[s] = (shift(add(*sums[s]), -s),)

    own_routes = lax.dynamic_slice_in_dim(routes, seq_place * count, count, 0)
    dy, x = {0: with_router(grad_out, own_routes, probs)}, {0: tokens}
    dy_side, x_side = {}, {}
    shifts = sorted(range(ring), key=lambda s: (min(s, ring - s), s))
    for s in shifts[1:]:
        dy[s] = shift(dy[0], s)
    dy_side[0] = across(dy[0])
    x_side[0] = across(x[0])
    done = []
    for s in shifts[1:]:
        dy_side[s] = across(after(dy[s], *done))
        compute(shifts[len(done)])
        done.append(slots[shifts[len(done)]])
    for s in range(1, ring):
        x[s] = shift(x[s - 1], 1)
    for s in shifts:
        if s not in slots:
            compute(s)
        give_back(s)
    for s in range(1, ring):
        x_side[s] = across(x[s])

    back = [term for s in shifts for term in sums[s]]
    total = add(*back)
    pieces = {0: [tokens, x_side[0], other_core(tokens), other_core(x_side[0])]}
    for s in range(1, ring):
        held, side_held = other_core(x[s]), other_core(x_side[s])
        pieces[s] = [x[s], x_side[s], held, side_held]
    first = after(rows[shifts[0]], *[slots[s] for s in shifts])
    grad_down = down_grad([scaled[s] for s in shifts], [first] + [rows[s] for s in shifts[1:]])
    grad_gate, grad_up = input_grads(
        width,
        [piece for s in shifts for piece in pieces[s]], *[[part[s] for s in shifts] for part in (dgu, slots)]
    )
    grad_probs = total[count:count + chosen, :count].T
    return (total[:count], grad_probs, grad_gate[None], grad_up[None], grad_down[None])


def local(tokens, grad_out, probs, routes, w_gate, w_up, w_down, gate_pre, up_pre):
    experts = lax.axis_size("seq") * lax.axis_size("expert")
    gathers = experts * tokens.shape[0] <= 2 * gate_pre.shape[1] and experts <= 256
    plan = gather_local if gathers and lax.axis_size("expert") == 4 else exchange_local
    return plan(tokens, grad_out, probs, routes, w_gate, w_up, w_down, gate_pre, up_pre)


def solution(mesh):
    return jax.shard_map(
        local,
        mesh=mesh,
        in_specs=(
            P(("group", "expert", "seq"), None),
            P(("group", "expert", "seq"), None),
            P(("group", "expert", "seq"), None),
            P(("group", "expert"), None),
            P(("expert", "seq"), None, None),
            P(("expert", "seq"), None, None),
            P(("expert", "seq"), None, None),
            P(("group", "expert", "seq"), None, None),
            P(("group", "expert", "seq"), None, None),
        ),
        out_specs=(
            P(("group", "expert", "seq"), None),
            P(("group", "expert", "seq"), None),
            P(("group", "expert", "seq"), None, None),
            P(("group", "expert", "seq"), None, None),
            P(("group", "expert", "seq"), None, None),
        ),
        check_vma=False,
    )
```
